32 devices in a mesh: ctx: 8 (over z, x), head: 4 (over y, core).
Axes of the slice: x: 2, y: 2, z: 4, core: 2. Of those that a mesh axis runs over, the one named last changes fastest.
Arguments:
- hidden: bfloat16 [8192, 1536], P('ctx', 'head'), may hold values from -6 to 6
- norm_gain: float32 [1536], replicated, may hold values from 0.1 to 1.9
- zx_weight: bfloat16 [1536, 2, 3072], P(None, None, 'head'), may hold values from -0.15625 to 0.15625
- bc_weight: bfloat16 [1536, 256], replicated, may hold values from -0.15625 to 0.15625
- dt_weight: bfloat16 [1536, 48], P(None, 'head'), may hold values from -0.15625 to 0.15625
- conv_x: float32 [5, 3072], P(None, 'head'), may hold values from -0.5 to 0.5
- conv_bc: float32 [5, 256], replicated, may hold values from -0.5 to 0.5
- dt_bias: float32 [48], P('head'), may hold values from -4.6 to -2.3
- log_decay: float32 [8192, 48], P('ctx', 'head'), may hold values from -1.5 to 0, as said below
- skip_gain: float32 [48], P('head'), may hold values from 0.5 to 2
- out_gain: float32 [3072], P('head'), may hold values from 0.1 to 1.9
- out_weight: bfloat16 [3072, 1536], P('head'), may hold values from -0.109375 to 0.109375
Outputs:
- mixed: bfloat16 [8192, 1536], P('ctx', 'head')
The draws below stay inside these ranges and needn't reach their ends.
Inputs may be any that keep to these rules, and one draw needn't show every extreme that they name: `log_decay`: negative everywhere; in some heads a token keeps only a few percent of the state after a few tens of positions, other heads decay over the whole document, and a head may lose a sizeable share of its state at single tokens.
All inputs are finite; a program needn't handle non-finite values.
Results may differ from the reference program's by a relative error of at most 0.015.
Values may be sent and summed in bfloat16 or wider, within the bound.
A program may use at most 128 MiB of HBM per device.

```python
import math
import jax
import jax.numpy as jnp
from jax import lax

D = 1536
HEAD_TOTAL = 48
HEADDIM = 64
STATE = 128
CONV = 4
BLOCK = 256
TOK_DEV = 1024
INNER = 3072
DOCUMENT_LENGTH = 8192
N_HEAD = 4


def draw_log_decay(key, part):
    random_subkeys = jax.random.split(key, 7)
    fast_share = 0.5
    is_fast = jax.random.uniform(random_subkeys[0], (HEAD_TOTAL,)) < fast_share
    fast_rate = 1.0 / jax.random.uniform(random_subkeys[1], (HEAD_TOTAL,), minval=30.0, maxval=50.0)
    slow_rate = jax.random.uniform(random_subkeys[2], (HEAD_TOTAL,), minval=0.2, maxval=0.6) / DOCUMENT_LENGTH
    base_rate = jnp.where(is_fast, fast_rate, slow_rate)
    blocks = DOCUMENT_LENGTH // TOK_DEV
    device_factor = jnp.exp(jax.random.uniform(random_subkeys[3], (blocks, 1, HEAD_TOTAL), minval=-0.4, maxval=0.4))
    token_factor = jnp.exp(jax.random.uniform(random_subkeys[4], (blocks, TOK_DEV, HEAD_TOTAL), minval=-0.7, maxval=0.7))
    decay_speed = (base_rate * device_factor * token_factor).reshape(DOCUMENT_LENGTH, HEAD_TOTAL)
    spike_position = jax.random.randint(random_subkeys[5], (2, HEAD_TOTAL), 0, DOCUMENT_LENGTH)
    spike_magnitude = jnp.log(jax.random.uniform(random_subkeys[6], (2, HEAD_TOTAL), minval=0.5, maxval=0.8))
    token_locations = jnp.arange(DOCUMENT_LENGTH)[:, None]
    spike_events = jnp.where(token_locations == spike_position[0], spike_magnitude[0], 0.0) + jnp.where(token_locations == spike_position[1], spike_magnitude[1], 0.0)
    return (spike_events - decay_speed).astype(jnp.float32)


def levels(rng, shape, cuts, least, top_value):
    def one(dim, parts):
        draws = jax.random.uniform(jax.random.fold_in(jax.random.fold_in(rng, 6), dim), (parts,), jnp.float32, least / len(cuts), top_value / len(cuts))
        return jnp.repeat(jnp.exp(draws), shape[dim] // parts).reshape((-1,) + (1,) * (len(shape) - dim - 1))

    level = one(*cuts[0])
    for cut in cuts[1:]:
        level = level * one(*cut)
    return level


def centred(rng, extent, scale, limit, pieces=(), kind=jnp.bfloat16):
    entries = jax.random.normal(rng, extent, jnp.float32) * scale
    if len(pieces) > 0:
        entries = levels(rng, extent, pieces, -0.22, 0.18) * entries
    return jnp.clip(entries, min=-limit, max=limit).astype(kind)


def setup_inputs(seed: int = 0) -> dict:
    seeds = jax.random.split(jax.random.key(seed), 13)
    return {
        "hidden": centred(seeds[0], (DOCUMENT_LENGTH, D), 1.0, 6.0, ((0, 8), (1, 4))),
        "norm_gain": jnp.clip(1.0 + 0.18 * jax.random.normal(seeds[1], (D,), jnp.float32), 0.1, 1.9),
        "zx_weight": centred(seeds[2], (D, 2, INNER), D ** -0.5, 0.15625, ((2, 4),)),
        "bc_weight": centred(seeds[3], (D, 2 * STATE), D ** -0.5, 0.15625),
        "dt_weight": centred(seeds[4], (D, HEAD_TOTAL), D ** -0.5, 0.15625, ((1, 4),)),
        "conv_x": jnp.clip(jax.random.uniform(seeds[5], (CONV + 1, INNER), jnp.float32, -0.5, 0.5) * levels(seeds[5], (CONV + 1, INNER), ((1, 4),), -0.4, 0.0), -0.5, 0.5),
        "conv_bc": jnp.clip(jax.random.uniform(seeds[6], (CONV + 1, 2 * STATE), jnp.float32, -0.5, 0.5), -0.5, 0.5),
        "dt_bias": jnp.clip(-4.6 + 2.3 * jax.random.uniform(seeds[7], (HEAD_TOTAL,), jnp.float32) ** levels(seeds[7], (HEAD_TOTAL,), ((0, 4),), -0.2, 0.2), -4.6, -2.3),
        "log_decay": draw_log_decay(jax.random.fold_in(seeds[12], 71), 0),
        "skip_gain": jnp.clip(jnp.exp(math.log(2.0) - 1.3862944 * jax.random.uniform(seeds[9], (HEAD_TOTAL,), jnp.float32) ** levels(seeds[9], (HEAD_TOTAL,), ((0, 4),), -0.2, 0.2)), 0.5, 2.0),
        "out_gain": jnp.clip(1.0 + 0.18 * jax.random.normal(seeds[10], (INNER,), jnp.float32), 0.1, 1.9),
        "out_weight": centred(seeds[11], (INNER, D), INNER ** -0.5, 0.109375, ((0, 4),)),
    }


eps = 1e-05

def convolve(extended, conv_taps):
    tap_count = conv_taps.shape[0] - 1
    out_rows = extended.shape[0] - tap_count + 1
    summed_taps = conv_taps[tap_count]
    for offset in range(tap_count):
        summed_taps = summed_taps + conv_taps[offset] * extended[offset:offset + out_rows].astype(jnp.float32)
    return jax.nn.silu(summed_taps).astype(jnp.bfloat16)

def reference(hidden, norm_gain, zx_weight, bc_weight, dt_weight, conv_x, conv_bc, dt_bias, log_decay, skip_gain, out_gain, out_weight):
    rim_rows = CONV - 1
    position = jnp.arange(BLOCK)
    causal = position[:, None] >= position[None, :]
    group_width = INNER // N_HEAD
    highest = lax.Precision.HIGHEST

    def advance(carry_in, block_in):
        previous_raw, state = carry_in
        row_block, decay_rows = block_in
        values = row_block.astype(jnp.float32)
        mean_square = lax.optimization_barrier(jnp.mean(values * values, axis=-1, keepdims=True))
        normed = (values * lax.rsqrt(mean_square + eps) * norm_gain).astype(jnp.bfloat16)
        gate_raw = jnp.dot(normed, zx_weight[:, 0, :], preferred_element_type=jnp.float32).astype(jnp.bfloat16)
        x_raw = jnp.dot(normed, zx_weight[:, 1, :], preferred_element_type=jnp.float32).astype(jnp.bfloat16)
        bc_raw = jnp.dot(normed, bc_weight, preferred_element_type=jnp.float32).astype(jnp.bfloat16)
        step_raw = jnp.dot(normed, dt_weight, preferred_element_type=jnp.float32).astype(jnp.bfloat16)
        projected = jnp.concatenate([x_raw, bc_raw], axis=1)
        extended = jnp.concatenate([previous_raw, projected], axis=0)
        x_conv = convolve(extended[:, :INNER], conv_x)
        bc_conv = convolve(extended[:, INNER:], conv_bc)
        b_rows = bc_conv[:, :STATE]
        c_rows = bc_conv[:, STATE:]
        step_size = jax.nn.softplus(step_raw.astype(jnp.float32) + dt_bias)
        decay_sum = jnp.cumsum(decay_rows, axis=0)
        decay_t = decay_sum.T
        step_t = step_size.T
        scores = jnp.dot(c_rows, b_rows.T, preferred_element_type=jnp.float32)
        log_gap = jnp.where(causal, decay_t[:, :, None] - decay_t[:, None, :], 0.0)
        mix_weights = jnp.where(causal, scores[None] * jnp.exp(log_gap) * step_t[:, None, :], 0.0).astype(jnp.bfloat16)
        x_heads = x_conv.reshape(BLOCK, HEAD_TOTAL, HEADDIM).astype(jnp.float32)
        y_inside = jnp.einsum('hts,shp->thp', mix_weights.astype(jnp.float32), x_heads, precision=highest)
        c_wide = c_rows.astype(jnp.float32)
        b_wide = b_rows.astype(jnp.float32)
        y_carried = jnp.exp(decay_sum)[:, :, None] * jnp.einsum('tn,hpn->thp', c_wide, state, precision=highest)
        to_end = jnp.exp(decay_t[:, -1:] - decay_t) * step_t
        weighted = x_heads * to_end.T[:, :, None]
        block_state = jnp.einsum('shp,sn->hpn', weighted, b_wide, precision=highest)
        new_state = jnp.exp(decay_t[:, -1])[:, None, None] * state + block_state
        y_heads = y_inside + y_carried + skip_gain[None, :, None] * x_heads
        gated = y_heads.reshape(BLOCK, INNER) * jax.nn.silu(gate_raw.astype(jnp.float32))
        square_mean = lax.optimization_barrier(jnp.mean(gated * gated, axis=-1, keepdims=True))
        y_normed = (gated * lax.rsqrt(square_mean + eps) * out_gain).astype(jnp.bfloat16)
        summed = jnp.zeros((BLOCK, D), jnp.float32)
        for group in range(N_HEAD):
            piece = jnp.dot(y_normed[:, group * group_width:(group + 1) * group_width], out_weight[group * group_width:(group + 1) * group_width], preferred_element_type=jnp.float32).astype(jnp.bfloat16)
            piece = lax.optimization_barrier(piece)
            summed = summed + piece.astype(jnp.float32)
        return ((extended[extended.shape[0] - rim_rows:], new_state), summed.astype(jnp.bfloat16))
    start_carry = (jnp.zeros((rim_rows, INNER + 2 * STATE), jnp.bfloat16), jnp.zeros((HEAD_TOTAL, HEADDIM, STATE), jnp.float32))
    block_total = DOCUMENT_LENGTH // BLOCK
    unused, outputs = lax.scan(advance, start_carry, (hidden.reshape(block_total, BLOCK, D), log_decay.reshape(block_total, BLOCK, HEAD_TOTAL)))
    return outputs.reshape(DOCUMENT_LENGTH, D)
```

```python
import functools

import jax
import jax.numpy as jnp
from jax import lax
from jax.experimental import pallas as pl
from jax.experimental.pallas import tpu as pltpu
from jax.sharding import PartitionSpec as P

HEADDIM = 64
STATE = 128
CONV = 4
BLOCK = 256
HALO = 16
QUAD = 256
GROUP = 128
PER = QUAD // HEADDIM
SUB = 128
LANES = 128
CUT = 256

eps = 1e-05
F32 = jnp.float32
BF16 = jnp.bfloat16


def dot(a, b):
    return jnp.dot(a, b, preferred_element_type=F32)


def silu(v):
    half = 0.5 * v
    return half + half * jnp.tanh(half)


def spread(column_of, first, lane, rows):
    out = None
    for k in range(PER):
        piece = jnp.broadcast_to(column_of(first + k), (rows, QUAD))
        out = piece if out is None else jnp.where(lane >= k * HEADDIM, piece, out)
    return out


def kernel(
    places,
    hidden,
    wzx_hbm,
    wbc_hbm,
    wout_hbm,
    gain,
    wdt_in,
    taps_x,
    taps_bc,
    dtb,
    ld_in,
    skip,
    out_gain,
    out,
    xg,
    wraw,
    wf,
    wzx,
    wbc,
    wout,
    wdt,
    dtrow,
    skrow,
    nrm,
    tail,
    ldp,
    xc,
    cm,
    yl,
    gr,
    ent,
    tl,
    et,
    dcol_all,
    ed,
    drow_all,
    st,
    dsum,
    sc_keep,
    sr_keep,
    got_d,
    dpair,
    got_dp,
    got_s,
    snd_s,
    got_e,
    got_t,
    snd_e,
    snd_b,
    back,
    inc,
    gb,
    send_p,
    recv_p,
    own,
    send_y,
    recv_y,
    sq_own,
    sq_p,
    sq_sum,
    sq_far,
    load_sem,
    ys,
    yr,
    ps,
    pr,
    fs,
    fr,
    hs,
    hr,
    ds_,
    dr_,
    cs,
    cr,
    es,
    er,
    ts,
    tr,
    bs,
    br,
    rs,
    rr,
    zs,
    zr,
    qs,
    qr,
):
    rows, feat = hidden.shape
    width = 4 * feat
    inner = wzx.shape[1] // 2
    heads = inner // HEADDIM
    quads = inner // QUAD
    chunks = rows // BLOCK
    subs = rows // SUB
    tiles = inner // LANES
    ctx = lax.axis_index("ctx")
    me = lax.axis_index("head")
    partner = me + 1 - 2 * lax.rem(me, 2)
    other = lax.rem(me + 2, 4)
    diag = lax.rem(partner + 2, 4)
    odd = lax.rem(ctx, 2)
    mate = ctx + 1 - 2 * odd
    pair = lax.div(ctx, 2)
    odd_pair = lax.rem(pair, 2)
    MESH = pl.DeviceIdType.MESH

    def remote(src, dst, ss, rsem, c, h):
        return pltpu.make_async_remote_copy(
            src_ref=src, dst_ref=dst, send_sem=ss, recv_sem=rsem, device_id=(c, h), device_id_type=MESH
        )

    def columns(h):
        return pl.ds(pl.multiple_of(h * feat, 128), feat)

    own_load = pltpu.make_async_copy(hidden, xg.at[me, pl.ds(HALO, rows)], load_sem.at[0])
    bc_load = pltpu.make_async_copy(wbc_hbm, wbc, load_sem.at[1])
    zx_loads = [
        pltpu.make_async_copy(
            wzx_hbm.at[:, :, pl.ds(j * LANES, LANES)], wraw.at[j], load_sem.at[6 + j]
        )
        for j in range(tiles)
    ]
    out_loads = [
        pltpu.make_async_copy(
            wout_hbm.at[:, columns(h)], wout.at[:, pl.ds(k * feat, feat)], load_sem.at[2 + k]
        )
        for k, h in enumerate((partner, diag, other, me))
    ]

    barrier = pltpu.get_barrier_semaphore()

    def greet(c, h):
        pl.semaphore_signal(barrier, inc=1, device_id=(c, h), device_id_type=MESH)

    for h in (partner, other, diag):
        greet(ctx, h)

    @pl.when(ctx > 0)
    def _():
        for h in range(4):
            greet(ctx - 1, h)

    @pl.when(ctx < places - 1)
    def _():
        for h in range(4):
            greet(ctx + 1, h)

    for gap in (2, 4):

        @pl.when(ctx >= gap)
        def _():
            greet(ctx - gap, me)

        @pl.when(ctx < places - gap)
        def _():
            greet(ctx + gap, me)

    own_load.start()
    for load in zx_loads:
        load.start()
    bc_load.start()
    for load in out_loads:
        load.start()

    lane = lax.broadcasted_iota(jnp.int32, (1, QUAD), 1)
    row_id = lax.broadcasted_iota(jnp.int32, (BLOCK, BLOCK), 0)
    col_id = lax.broadcasted_iota(jnp.int32, (BLOCK, BLOCK), 1)

    dt_wide = jnp.concatenate(
        [wdt_in[...].astype(F32), jnp.zeros((128 - heads, width), F32)], axis=0
    )
    wdt[...] = dt_wide.T.astype(BF16)
    few = lax.broadcasted_iota(jnp.int32, (8, 128), 1)
    bias_row = jnp.zeros((8, 128), F32)
    for h in range(heads):
        bias_row = jnp.where(few == h, dtb[h], bias_row)
    dtrow[...] = bias_row
    wide = lax.broadcasted_iota(jnp.int32, (8, inner), 1)
    skip_row = jnp.zeros((8, inner), F32)
    for h in range(heads):
        skip_row = jnp.where(wide >= h * HEADDIM, skip[h], skip_row)
    skrow[...] = skip_row
    st[...] = jnp.zeros_like(st)
    dsum[...] = jnp.zeros_like(dsum)
    ldp[...] = jnp.zeros_like(ldp)
    tri = jnp.where(row_id <= col_id, 1.0, 0.0).astype(F32)

    def decays(c, carry):
        here = pl.ds(pl.multiple_of(c * BLOCK, BLOCK), BLOCK)
        ldp[0:heads, :] = ld_in[:, here]
        drow = jnp.dot(ldp[...], tri, preferred_element_type=F32, precision=lax.Precision.HIGHEST)
        dcol = jnp.concatenate([drow, jnp.zeros((112, BLOCK), F32)], axis=0).T
        drow_all[c] = drow
        dcol_all[here, :] = dcol
        ed[here, :] = jnp.exp(dcol)
        tl[c] = dsum[...]
        for q in range(quads):
            span = slice(q * QUAD, (q + 1) * QUAD)
            total = spread(lambda i: dcol[BLOCK - 1 : BLOCK, i : i + 1], q * PER, lane, 1)
            et[c, :, span] = jnp.broadcast_to(jnp.exp(total), (8, QUAD))
            dsum[:, span] = dsum[:, span] + total
        return carry

    lax.fori_loop(0, chunks, decays, 0)

    def split(j):
        flat = wraw.at[j].reshape(2 * width, LANES)

        def step(i, carry):
            for u in range(2):
                at = pl.multiple_of((2 * i + u) * CUT, CUT)
                wf[u] = flat[pl.ds(pl.multiple_of(2 * at, 2 * CUT), 2 * CUT), :].astype(F32)
                for g in range(2):
                    first = g * inner + j * LANES
                    wzx[pl.ds(at, CUT), first : first + LANES] = wf[
                        u, pl.ds(g, CUT, stride=2), :
                    ].astype(BF16)
            return carry

        lax.fori_loop(0, width // (2 * CUT), step, 0)

    early = 2
    for j in range(early):
        zx_loads[j].wait()
        split(j)

    below = lax.div(ctx + places - 1, places)
    above = lax.div(2 * places - 2 - ctx, places)
    hops = 0
    for gap in (2, 4):
        hops = hops + lax.div(ctx + places - gap, places)
        hops = hops + lax.div(2 * places - 1 - gap - ctx, places)
    pl.semaphore_wait(barrier, 3 + 4 * (below + above) + hops)

    def src_rows(c):
        return hidden.at[pl.ds(pl.multiple_of(c * BLOCK, BLOCK), BLOCK)]

    def slot(h, c):
        return xg.at[h, pl.ds(pl.multiple_of(HALO + c * BLOCK, HALO), BLOCK)]

    def to_y(c):
        return remote(src_rows(c), slot(me, c), ys.at[c], yr.at[c], ctx, other)

    def to_p(c):
        return remote(src_rows(c), slot(me, c), ps.at[c], pr.at[c], ctx, partner)

    def forward(c):
        return remote(slot(other, c), slot(other, c), fs.at[c], fr.at[c], ctx, partner)

    def forwarded(c):
        return remote(slot(diag, c), slot(diag, c), fs.at[c], fr.at[c], ctx, partner)

    def halo(h, sender):
        return remote(
            hidden.at[pl.ds(rows - HALO, HALO)],
            xg.at[sender, pl.ds(0, HALO)],
            hs.at[h],
            hr.at[sender],
            ctx + 1,
            h,
        )

    decay_copy = remote(dsum, got_d, ds_.at[0], dr_.at[0], mate, me)
    decay_pair_copy = remote(dpair, got_dp, ds_.at[1], dr_.at[1], ctx + 2, me)

    @pl.when(ctx < places - 1)
    def _():
        for h in range(4):
            halo(h, me).start()

    for c in range(chunks):
        to_y(c).start()
    for c in range(chunks):
        to_p(c).start()
    decay_copy.start()

    @pl.when(ctx == 0)
    def _():
        xg[:, 0:HALO, :] = jnp.zeros((4, HALO, feat), BF16)

    for j in range(early, tiles):
        zx_loads[j].wait()
        split(j)

    bc_load.wait()
    own_load.wait()
    decay_copy.wait_recv()
    dpair[...] = dsum[...] + got_d[...]

    @pl.when(ctx < places - 2)
    def _():
        decay_pair_copy.start()

    @pl.when(ctx > 0)
    def _():
        for h in range(4):
            halo(0, h).wait_recv()

    def normalised(at, count):
        vals = [xg[j, at, :].astype(F32) for j in range(4)]
        total = sum(jnp.sum(v * v, axis=-1, keepdims=True) for v in vals)
        scale = lax.rsqrt(total / width + eps)
        return [
            (vals[j] * scale * gain[j * feat : (j + 1) * feat].reshape(1, feat)).astype(BF16)
            for j in range(4)
        ]

    head_rows = jnp.concatenate(normalised(pl.ds(0, HALO), HALO), axis=1)
    for s in range(quads):
        tail[:, s * QUAD : (s + 1) * QUAD] = dot(
            head_rows, wzx[:, inner + s * QUAD : inner + (s + 1) * QUAD]
        )
    tail[:, inner : inner + 2 * STATE] = dot(head_rows, wbc[...])

    def convolved(raw, span, taps):
        ext = jnp.concatenate([tail[:, span], raw], axis=0)
        summed = taps[CONV : CONV + 1, :] + taps[CONV - 1 : CONV, :] * ext
        for back_by in range(1, CONV):
            at = CONV - 1 - back_by
            summed = summed + taps[at : at + 1, :] * pltpu.roll(ext, back_by, 0)
        tail[:, span] = raw[BLOCK - HALO :, :]
        return silu(summed[HALO:, :])

    def inside(c):
        here = pl.ds(pl.multiple_of(c * BLOCK, BLOCK), BLOCK)
        scores = sc_keep[...]
        cc = cm[here, :]
        for q in range(quads):
            span = slice(q * QUAD, (q + 1) * QUAD)
            xq = xc[here, span]
            mixes = []
            parts = []
            for k in range(PER):
                h = q * PER + k
                gap = jnp.minimum(
                    dcol_all[here, h : h + 1] - drow_all[c, h : h + 1, :], 0.0
                )
                mixes.append((scores * jnp.exp(gap) * sr_keep[h : h + 1, :]).astype(BF16))
                mine = (lane >= k * HEADDIM) & (lane < (k + 1) * HEADDIM)
                parts.append(jnp.where(mine, xq, jnp.zeros_like(xq)))
            y = dot(jnp.concatenate(mixes, axis=1), jnp.concatenate(parts, axis=0))
            growth = spread(lambda i: ed[here, i : i + 1], q * PER, lane, BLOCK)
            y = y + growth * dot(cc, ent[c, :, span])
            yl[here, span] = y + skrow[0:1, span] * xq.astype(F32)
            gr[here, span] = growth * jnp.exp(tl[c, 0:1, span])

    def gates(c):
        here = pl.ds(pl.multiple_of(c * BLOCK, BLOCK), BLOCK)
        normed = nrm[here, :]
        for q in range(quads):
            span = slice(q * QUAD, (q + 1) * QUAD)
            g = silu(dot(normed, wzx[:, span]))
            yl[here, span] = yl[here, span] * g
            gr[here, span] = gr[here, span] * g

    def first(c, carry):
        @pl.when(c > 0)
        def _():
            inside(c - 1)

        to_y(c).wait_recv()
        forward(c).start()
        to_p(c).wait_recv()
        forwarded(c).wait_recv()
        here = pl.ds(pl.multiple_of(c * BLOCK, BLOCK), BLOCK)
        pieces = normalised(pl.ds(pl.multiple_of(HALO + c * BLOCK, HALO), BLOCK), BLOCK)
        for j in range(4):
            nrm[here, j * feat : (j + 1) * feat] = pieces[j]
        normed = nrm[here, :]
        bc = convolved(dot(normed, wbc[...]), slice(inner, inner + 2 * STATE), taps_bc[...])
        b = bc[:, :STATE].astype(BF16)
        cc = bc[:, STATE:].astype(BF16)
        cm[here, :] = cc
        raw_step = dot(normed, wdt[...]) + dtrow[0:1, :]
        step = jnp.maximum(raw_step, 0.0) + jnp.log1p(jnp.exp(-jnp.abs(raw_step)))
        srow = step.T[0:16, :]
        drow = drow_all[c]
        wrow = jnp.exp(drow[:, BLOCK - 1 : BLOCK] - drow) * srow
        sr_keep[...] = srow
        scores = lax.dot_general(cc, b, (((1,), (1,)), ((), ())), preferred_element_type=F32)
        sc_keep[...] = jnp.where(row_id >= col_id, scores, 0.0)
        b_t = b.astype(F32).T
        for q in range(quads):
            span = slice(q * QUAD, (q + 1) * QUAD)
            raw = dot(normed, wzx[:, inner + q * QUAD : inner + (q + 1) * QUAD])
            xq = convolved(raw, span, taps_x[:, span]).astype(BF16)
            xc[here, span] = xq
            s_acc = None
            for k in range(PER):
                h = q * PER + k
                wb = (b_t * wrow[h : h + 1, :]).astype(BF16)
                s_h = dot(wb, xq)
                s_acc = s_h if k == 0 else jnp.where(lane >= k * HEADDIM, s_h, s_acc)
            ent[c, :, span] = st[:, span].astype(BF16)
            st[:, span] = et[c, 0:1, span] * st[:, span] + s_acc
        return carry

    lax.fori_loop(0, chunks, first, 0)

    turns = inner // GROUP // 2

    def lanes_of(g):
        return pl.ds(pl.multiple_of(g * GROUP, GROUP), GROUP)

    def state_copy(i):
        return remote(snd_s.at[i], got_s.at[i], cs.at[i], cr.at[i], mate, me)

    def enter_copy(i):
        return remote(snd_e.at[i], got_e.at[i], es.at[i], er.at[i], ctx + 2, me)

    def leap_copy(i):
        return remote(snd_e.at[i], got_t.at[i], ts.at[i], tr.at[i], ctx + 4, me)

    def back_copy(i):
        return remote(snd_b.at[i], back.at[i], bs.at[i], br.at[i], mate, me)

    def pair_parts(i):
        at = lanes_of(2 * i + odd)
        mine, theirs = st[:, at], got_s[i].astype(F32)
        earlier = jnp.where(odd == 0, mine, theirs)
        later = jnp.where(odd == 0, theirs, mine)
        d_earlier = jnp.where(odd == 0, dsum[0:1, at], got_d[0:1, at])
        d_later = jnp.where(odd == 0, got_d[0:1, at], dsum[0:1, at])
        return at, earlier, later, d_earlier, d_later

    def hand_back(i, at, entered, earlier, d_earlier):
        after = jnp.exp(d_earlier) * entered + earlier
        snd_b[i] = jnp.where(odd == 0, after, entered).astype(BF16)
        inc[:, at] = jnp.where(odd == 0, entered, after).astype(BF16)
        back_copy(i).start()

    def relay_even():
        for i in range(turns):
            state_copy(i).wait_recv()
            at, earlier, later, d_earlier, d_later = pair_parts(i)

            @pl.when(ctx < places - 2)
            def _():
                snd_e[i] = (jnp.exp(d_later) * earlier + later).astype(BF16)
                enter_copy(i).start()

    def finish_even():
        for i in range(turns):

            @pl.when(pair > 0)
            def _():
                enter_copy(i).wait_recv()

            at, earlier, later, d_earlier, d_later = pair_parts(i)
            hand_back(i, at, got_e[i].astype(F32), earlier, d_earlier)

    def relay_odd():
        for i in range(turns):
            state_copy(i).wait_recv()
            enter_copy(i).wait_recv()
            at, earlier, later, d_earlier, d_later = pair_parts(i)

            @pl.when(pair > 1)
            def _():
                leap_copy(i).wait_recv()

            entered = jnp.exp(got_dp[0:1, at]) * got_t[i].astype(F32) + got_e[i].astype(F32)

            @pl.when(ctx < places - 2)
            def _():
                whole = jnp.exp(d_earlier + d_later) * entered + jnp.exp(d_later) * earlier + later
                snd_e[i] = whole.astype(BF16)
                enter_copy(i).start()

            @pl.when(ctx < places - 4)
            def _():
                leap_copy(i).start()

            hand_back(i, at, entered, earlier, d_earlier)

    for i in range(turns):
        snd_s[i] = st[:, lanes_of(2 * i + 1 - odd)].astype(BF16)
        state_copy(i).start()

    @pl.when(ctx >= 2)
    def _():
        decay_pair_copy.wait_recv()

    @pl.when(ctx < 2)
    def _():
        got_e[...] = jnp.zeros_like(got_e)
        got_dp[...] = jnp.zeros_like(got_dp)

    @pl.when(pair <= 1)
    def _():
        got_t[...] = jnp.zeros_like(got_t)

    inside(chunks - 1)

    @pl.when(odd_pair == 0)
    def _():
        relay_even()

    half = chunks // 2

    def gate_step(c, carry):
        gates(c)
        return carry

    lax.fori_loop(0, half, gate_step, 0)

    @pl.when(pair == 1)
    def _():
        relay_odd()

    lax.fori_loop(half, chunks, gate_step, 0)

    @pl.when((odd_pair == 1) & (pair > 1))
    def _():
        relay_odd()

    @pl.when(odd_pair == 0)
    def _():
        finish_even()

    for load in out_loads:
        load.wait()

    for i in range(turns):
        back_copy(i).wait_recv()
        inc[:, lanes_of(2 * i + 1 - odd)] = back[i]

    def piece_copy(s):
        return remote(send_p.at[s], recv_p.at[s], rs.at[s], rr.at[s], ctx, partner)

    def far_copy(s):
        return remote(send_y.at[s], recv_y.at[s], zs.at[s], zr.at[s], ctx, other)

    def square_near(s):
        return remote(sq_own.at[s], sq_p.at[s], qs.at[0, s], qr.at[0, s], ctx, partner)

    def square_far(s):
        return remote(sq_sum.at[s], sq_far.at[s], qs.at[1, s], qr.at[1, s], ctx, other)

    def second(s, carry):
        here = pl.ds(pl.multiple_of(s * SUB, SUB), SUB)
        squares = jnp.zeros((SUB, 1), F32)
        cc = cm[here, :]
        for q in range(quads):
            span = slice(q * QUAD, (q + 1) * QUAD)
            gated = yl[here, span] + gr[here, span] * dot(cc, inc[:, span])
            squares = squares + jnp.sum(gated * gated, axis=-1, keepdims=True)
            gb[:, span] = (gated * out_gain[span].reshape(1, QUAD)).astype(BF16)
        g = gb[...]
        send_p[s] = dot(g, wout[:, 0 : 2 * feat]).astype(BF16)
        piece_copy(s).start()
        sq_own[s] = jnp.broadcast_to(squares, (SUB, 128)).T[0:8, :]
        square_near(s).start()
        own[s] = dot(g, wout[:, 2 * feat : 4 * feat])
        piece_copy(s).wait_recv()
        send_y[s] = (own[s, :, 0:feat] + recv_p[s, :, feat : 2 * feat].astype(F32)).astype(BF16)
        far_copy(s).start()
        square_near(s).wait_recv()
        sq_sum[s] = sq_own[s] + sq_p[s]
        square_far(s).start()
        own[s, :, feat : 2 * feat] = own[s, :, feat : 2 * feat] + recv_p[s, :, 0:feat].astype(F32)
        return carry

    lax.fori_loop(0, subs, second, 0)

    def third(s, carry):
        here = pl.ds(pl.multiple_of(s * SUB, SUB), SUB)
        square_far(s).wait_recv()
        scale_row = lax.rsqrt((sq_sum[s] + sq_far[s]) / (4 * inner) + eps)
        scale = jnp.broadcast_to(scale_row[0:1, :], (128, SUB)).T[:, 0:1]
        far_copy(s).wait_recv()
        out[here, :] = (
            (own[s, :, feat : 2 * feat] + recv_y[s].astype(F32)) * scale
        ).astype(BF16)
        return carry

    lax.fori_loop(0, subs, third, 0)

    for c in range(chunks):
        to_y(c).wait_send()
        to_p(c).wait_send()
        forward(c).wait_send()

    decay_copy.wait_send()
    for i in range(turns):
        state_copy(i).wait_send()
        back_copy(i).wait_send()

    @pl.when(ctx < places - 2)
    def _():
        decay_pair_copy.wait_send()
        for i in range(turns):
            enter_copy(i).wait_send()

    @pl.when((odd_pair == 1) & (ctx < places - 4))
    def _():
        for i in range(turns):
            leap_copy(i).wait_send()

    def drain(s, carry):
        piece_copy(s).wait_send()
        square_near(s).wait_send()
        far_copy(s).wait_send()
        square_far(s).wait_send()
        return carry

    lax.fori_loop(0, subs, drain, 0)

    @pl.when(ctx < places - 1)
    def _():
        for h in range(4):
            halo(h, me).wait_send()


def per_device(
    places,
    hidden,
    norm_gain,
    zx_weight,
    bc_weight,
    dt_weight,
    conv_x,
    conv_bc,
    dt_bias,
    log_decay,
    skip_gain,
    out_gain,
    out_weight,
):
    rows, feat = hidden.shape
    width = zx_weight.shape[0]
    inner = zx_weight.shape[2]
    turns = inner // GROUP // 2
    tiles = inner // LANES
    chunks = rows // BLOCK
    subs = rows // SUB
    any_spec = pl.BlockSpec(memory_space=pl.ANY)
    vmem = pl.BlockSpec(memory_space=pltpu.VMEM)
    smem = pl.BlockSpec(memory_space=pltpu.SMEM)
    dma = pltpu.SemaphoreType.DMA
    return pl.pallas_call(
        functools.partial(kernel, places),
        out_shape=jax.ShapeDtypeStruct((rows, feat), BF16),
        in_specs=[any_spec] * 4 + [vmem] * 4 + [smem, vmem, smem, vmem],
        out_specs=vmem,
        scratch_shapes=[
            pltpu.VMEM((4, HALO + rows, feat), BF16),
            pltpu.VMEM((tiles, width, 2, LANES), BF16),
            pltpu.VMEM((2, 2 * CUT, LANES), F32),
            pltpu.VMEM((width, 2 * inner), BF16),
            pltpu.VMEM((width, 2 * STATE), BF16),
            pltpu.VMEM((inner, width), BF16),
            pltpu.VMEM((width, 128), BF16),
            pltpu.VMEM((8, 128), F32),
            pltpu.VMEM((8, inner), F32),
            pltpu.VMEM((rows, width), BF16),
            pltpu.VMEM((HALO, inner + 2 * STATE), F32),
            pltpu.VMEM((16, BLOCK), F32),
            pltpu.VMEM((rows, inner), BF16),
            pltpu.VMEM((rows, STATE), BF16),
            pltpu.VMEM((rows, inner), F32),
            pltpu.VMEM((rows, inner), F32),
            pltpu.VMEM((chunks, STATE, inner), BF16),
            pltpu.VMEM((chunks, 8, inner), F32),
            pltpu.VMEM((chunks, 8, inner), F32),
            pltpu.VMEM((rows, 128), F32),
            pltpu.VMEM((rows, 128), F32),
            pltpu.VMEM((chunks, 16, BLOCK), F32),
            pltpu.VMEM((STATE, inner), F32),
            pltpu.VMEM((8, inner), F32),
            pltpu.VMEM((BLOCK, BLOCK), F32),
            pltpu.VMEM((16, BLOCK), F32),
            pltpu.VMEM((8, inner), F32),
            pltpu.VMEM((8, inner), F32),
            pltpu.VMEM((8, inner), F32),
            pltpu.VMEM((turns, STATE, GROUP), BF16),
            pltpu.VMEM((turns, STATE, GROUP), BF16),
            pltpu.VMEM((turns, STATE, GROUP), BF16),
            pltpu.VMEM((turns, STATE, GROUP), BF16),
            pltpu.VMEM((turns, STATE, GROUP), BF16),
            pltpu.VMEM((turns, STATE, GROUP), BF16),
            pltpu.VMEM((turns, STATE, GROUP), BF16),
            pltpu.VMEM((STATE, inner), BF16),
            pltpu.VMEM((SUB, inner), BF16),
            pltpu.VMEM((subs, SUB, 2 * feat), BF16),
            pltpu.VMEM((subs, SUB, 2 * feat), BF16),
            pltpu.VMEM((subs, SUB, 2 * feat), F32),
            pltpu.VMEM((subs, SUB, feat), BF16),
            pltpu.VMEM((subs, SUB, feat), BF16),
            pltpu.VMEM((subs, 8, SUB), F32),
            pltpu.VMEM((subs, 8, SUB), F32),
            pltpu.VMEM((subs, 8, SUB), F32),
            pltpu.VMEM((subs, 8, SUB), F32),
            dma((6 + tiles,)),
            dma((chunks,)),
            dma((chunks,)),
            dma((chunks,)),
            dma((chunks,)),
            dma((chunks,)),
            dma((chunks,)),
            dma((4,)),
            dma((4,)),
            dma((2,)),
            dma((2,)),
            dma((turns,)),
            dma((turns,)),
            dma((turns,)),
            dma((turns,)),
            dma((turns,)),
            dma((turns,)),
            dma((turns,)),
            dma((turns,)),
            dma((subs,)),
            dma((subs,)),
            dma((subs,)),
            dma((subs,)),
            dma((2, subs)),
            dma((2, subs)),
        ],
        compiler_params=pltpu.CompilerParams(
            collective_id=0, has_side_effects=True, vmem_limit_bytes=63000000
        ),
        name="mixer",
    )(
        hidden,
        zx_weight,
        bc_weight,
        out_weight,
        norm_gain,
        dt_weight.T,
        conv_x,
        conv_bc,
        dt_bias,
        log_decay.T,
        skip_gain,
        out_gain,
    )


def solution(mesh):
    placed = (
        P("ctx", "head"),
        P(),
        P(None, None, "head"),
        P(),
        P(None, "head"),
        P(None, "head"),
        P(),
        P("head"),
        P("ctx", "head"),
        P("head"),
        P("head"),
        P("head", None),
    )
    return jax.shard_map(
        functools.partial(per_device, mesh.shape["ctx"]),
        mesh=mesh,
        in_specs=placed,
        out_specs=P("ctx", "head"),
        check_vma=False,
    )
```

```python
import functools

import jax
import jax.numpy as jnp
from jax import lax
from jax.experimental import pallas as pl
from jax.experimental.pallas import tpu as pltpu
from jax.sharding import PartitionSpec as P

HEADDIM = 64
STATE = 128
CONV = 4
BLOCK = 256
HALO = 16
QUAD = 256
GROUP = 128
PER = QUAD // HEADDIM
SUB = 128
HALF = BLOCK // 2
LANES = 128
CUT = 256

eps = 1e-05
F32 = jnp.float32
BF16 = jnp.bfloat16


def dot(a, b):
    return jnp.dot(a, b, preferred_element_type=F32)


def silu(v):
    half = 0.5 * v
    return half + half * jnp.tanh(half)


def spread(column_of, first, lane, rows):
    out = None
    for k in range(PER):
        piece = jnp.broadcast_to(column_of(first + k), (rows, QUAD))
        out = piece if out is None else jnp.where(lane >= k * HEADDIM, piece, out)
    return out


def kernel(
    places,
    hidden,
    wzx_hbm,
    wbc_hbm,
    wout_hbm,
    gain,
    wdt_in,
    taps_x,
    taps_bc,
    dtb,
    ld_in,
    skip,
    out_gain,
    out,
    xg,
    wraw,
    wf,
    wzx,
    wbc,
    wout,
    wdt,
    dtrow,
    skrow,
    nrm,
    tail,
    ldp,
    xc,
    cm,
    yl,
    gr,
    ent,
    tl,
    et,
    dcol_all,
    expand,
    drow_all,
    st,
    dsum,
    sc_keep,
    e_keep,
    got_d,
    dpair,
    got_dp,
    got_s,
    snd_s,
    got_e,
    got_t,
    snd_e,
    snd_b,
    back,
    inc,
    gb,
    send_p,
    recv_p,
    own,
    send_y,
    recv_y,
    sq_own,
    sq_p,
    sq_sum,
    sq_far,
    load_sem,
    ys,
    yr,
    ps,
    pr,
    fs,
    fr,
    hs,
    hr,
    ds_,
    dr_,
    cs,
    cr,
    es,
    er,
    ts,
    tr,
    bs,
    br,
    rs,
    rr,
    zs,
    zr,
    qs,
    qr,
):
    rows, feat = hidden.shape
    width = 4 * feat
    inner = wzx.shape[1] // 2
    heads = inner // HEADDIM
    quads = inner // QUAD
    chunks = rows // BLOCK
    subs = rows // SUB
    tiles = inner // LANES
    ctx = lax.axis_index("ctx")
    me = lax.axis_index("head")
    partner = me + 1 - 2 * lax.rem(me, 2)
    other = lax.rem(me + 2, 4)
    diag = lax.rem(partner + 2, 4)
    odd = lax.rem(ctx, 2)
    mate = ctx + 1 - 2 * odd
    pair = lax.div(ctx, 2)
    odd_pair = lax.rem(pair, 2)
    MESH = pl.DeviceIdType.MESH

    def remote(src, dst, ss, rsem, c, h):
        return pltpu.make_async_remote_copy(
            src_ref=src, dst_ref=dst, send_sem=ss, recv_sem=rsem, device_id=(c, h), device_id_type=MESH
        )

    def columns(h):
        return pl.ds(pl.multiple_of(h * feat, 128), feat)

    own_load = pltpu.make_async_copy(hidden, xg.at[me, pl.ds(HALO, rows)], load_sem.at[0])
    bc_load = pltpu.make_async_copy(wbc_hbm, wbc, load_sem.at[1])
    zx_loads = [
        pltpu.make_async_copy(
            wzx_hbm.at[:, :, pl.ds(j * LANES, LANES)], wraw.at[j], load_sem.at[6 + j]
        )
        for j in range(tiles)
    ]
    out_loads = [
        pltpu.make_async_copy(
            wout_hbm.at[:, columns(h)], wout.at[:, pl.ds(k * feat, feat)], load_sem.at[2 + k]
        )
        for k, h in enumerate((partner, diag, other, me))
    ]

    barrier = pltpu.get_barrier_semaphore()

    def greet(c, h):
        pl.semaphore_signal(barrier, inc=1, device_id=(c, h), device_id_type=MESH)

    for h in (partner, other, diag):
        greet(ctx, h)

    @pl.when(ctx > 0)
    def _():
        for h in range(4):
            greet(ctx - 1, h)

    @pl.when(ctx < places - 1)
    def _():
        for h in range(4):
            greet(ctx + 1, h)

    for gap in (2, 4):

        @pl.when(ctx >= gap)
        def _():
            greet(ctx - gap, me)

        @pl.when(ctx < places - gap)
        def _():
            greet(ctx + gap, me)

    own_load.start()
    for load in zx_loads:
        load.start()
    bc_load.start()
    for load in out_loads:
        load.start()

    lane = lax.broadcasted_iota(jnp.int32, (1, QUAD), 1)
    row_id = lax.broadcasted_iota(jnp.int32, (BLOCK, BLOCK), 0)
    col_id = lax.broadcasted_iota(jnp.int32, (BLOCK, BLOCK), 1)

    def widened(per_head):
        high = per_head.astype(BF16).astype(F32)
        stack = jnp.concatenate([high, per_head - high, jnp.zeros((96, BLOCK), F32)], axis=0)
        return stack.T.astype(BF16)

    def split(j):
        flat = wraw.at[j].reshape(2 * width, LANES)

        def step(i, carry):
            for u in range(2):
                at = pl.multiple_of((2 * i + u) * CUT, CUT)
                wf[u] = flat[pl.ds(pl.multiple_of(2 * at, 2 * CUT), 2 * CUT), :].astype(F32)
                for g in range(2):
                    first = g * inner + j * LANES
                    wzx[pl.ds(at, CUT), first : first + LANES] = wf[
                        u, pl.ds(g, CUT, stride=2), :
                    ].astype(BF16)
            return carry

        lax.fori_loop(0, width // (2 * CUT), step, 0)

    dt_wide = jnp.concatenate(
        [wdt_in[...].astype(F32), jnp.zeros((128 - heads, width), F32)], axis=0
    )
    wdt[...] = dt_wide.T.astype(BF16)
    few = lax.broadcasted_iota(jnp.int32, (8, 128), 1)
    bias_row = jnp.zeros((8, 128), F32)
    for h in range(heads):
        bias_row = jnp.where(few == h, dtb[h], bias_row)
    dtrow[...] = bias_row
    wide = lax.broadcasted_iota(jnp.int32, (8, inner), 1)
    skip_row = jnp.zeros((8, inner), F32)
    for h in range(heads):
        skip_row = jnp.where(wide >= h * HEADDIM, skip[h], skip_row)
    skrow[...] = skip_row
    which = lax.broadcasted_iota(jnp.int32, (128, inner), 0)
    which = jnp.where(which >= 16, which - 16, which)
    across = lax.broadcasted_iota(jnp.int32, (128, inner), 1)
    within = (across >= which * HEADDIM) & (across < (which + 1) * HEADDIM)
    expand[...] = jnp.where(within, 1.0, 0.0).astype(BF16)
    st[...] = jnp.zeros_like(st)
    dsum[...] = jnp.zeros_like(dsum)
    ldp[...] = jnp.zeros_like(ldp)
    tri = jnp.where(row_id <= col_id, 1.0, 0.0).astype(F32)

    def decays(c, carry):
        here = pl.ds(pl.multiple_of(c * BLOCK, BLOCK), BLOCK)
        ldp[0:heads, :] = ld_in[:, here]
        drow = jnp.dot(ldp[...], tri, preferred_element_type=F32, precision=lax.Precision.HIGHEST)
        dcol = jnp.concatenate([drow, jnp.zeros((112, BLOCK), F32)], axis=0).T
        drow_all[c] = drow
        dcol_all[here, :] = dcol
        tl[c] = dsum[...]
        for q in range(quads):
            span = slice(q * QUAD, (q + 1) * QUAD)
            total = spread(lambda i: dcol[BLOCK - 1 : BLOCK, i : i + 1], q * PER, lane, 1)
            et[c, :, span] = jnp.broadcast_to(jnp.exp(total), (8, QUAD))
            dsum[:, span] = dsum[:, span] + total
        return carry

    lax.fori_loop(0, chunks, decays, 0)

    below = lax.div(ctx + places - 1, places)
    above = lax.div(2 * places - 2 - ctx, places)
    hops = 0
    for gap in (2, 4):
        hops = hops + lax.div(ctx + places - gap, places)
        hops = hops + lax.div(2 * places - 1 - gap - ctx, places)
    pl.semaphore_wait(barrier, 3 + 4 * (below + above) + hops)

    def src_rows(c):
        return hidden.at[pl.ds(pl.multiple_of(c * BLOCK, BLOCK), BLOCK)]

    def slot(h, c):
        return xg.at[h, pl.ds(pl.multiple_of(HALO + c * BLOCK, HALO), BLOCK)]

    def to_y(c):
        return remote(src_rows(c), slot(me, c), ys.at[c], yr.at[c], ctx, other)

    def to_p(c):
        return remote(src_rows(c), slot(me, c), ps.at[c], pr.at[c], ctx, partner)

    def forward(c):
        return remote(slot(other, c), slot(other, c), fs.at[c], fr.at[c], ctx, partner)

    def forwarded(c):
        return remote(slot(diag, c), slot(diag, c), fs.at[c], fr.at[c], ctx, partner)

    def halo(h, sender):
        return remote(
            hidden.at[pl.ds(rows - HALO, HALO)],
            xg.at[sender, pl.ds(0, HALO)],
            hs.at[h],
            hr.at[sender],
            ctx + 1,
            h,
        )

    decay_copy = remote(dsum, got_d, ds_.at[0], dr_.at[0], mate, me)
    decay_pair_copy = remote(dpair, got_dp, ds_.at[1], dr_.at[1], ctx + 2, me)

    @pl.when(ctx < places - 1)
    def _():
        for h in range(4):
            halo(h, me).start()

    for c in range(chunks):
        to_y(c).start()
    for c in range(chunks):
        to_p(c).start()

    @pl.when(ctx == 0)
    def _():
        xg[:, 0:HALO, :] = jnp.zeros((4, HALO, feat), BF16)

    decay_copy.start()

    for j in range(tiles):
        zx_loads[j].wait()
        split(j)

    bc_load.wait()
    own_load.wait()
    decay_copy.wait_recv()
    dpair[...] = dsum[...] + got_d[...]

    @pl.when(ctx < places - 2)
    def _():
        decay_pair_copy.start()

    @pl.when(ctx > 0)
    def _():
        for h in range(4):
            halo(0, h).wait_recv()

    def normalised(at, count):
        vals = [xg[j, at, :].astype(F32) for j in range(4)]
        total = sum(jnp.sum(v * v, axis=-1, keepdims=True) for v in vals)
        scale = lax.rsqrt(total / width + eps)
        return [
            (vals[j] * scale * gain[j * feat : (j + 1) * feat].reshape(1, feat)).astype(BF16)
            for j in range(4)
        ]

    head_rows = jnp.concatenate(normalised(pl.ds(0, HALO), HALO), axis=1)
    for s in range(quads):
        tail[:, s * QUAD : (s + 1) * QUAD] = dot(
            head_rows, wzx[:, inner + s * QUAD : inner + (s + 1) * QUAD]
        )
    tail[:, inner : inner + 2 * STATE] = dot(head_rows, wbc[...])

    def convolved(raw, span, taps):
        ext = jnp.concatenate([tail[:, span], raw], axis=0)
        summed = taps[CONV : CONV + 1, :] + taps[CONV - 1 : CONV, :] * ext
        for back_by in range(1, CONV):
            at = CONV - 1 - back_by
            summed = summed + taps[at : at + 1, :] * pltpu.roll(ext, back_by, 0)
        tail[:, span] = raw[BLOCK - HALO :, :]
        return silu(summed[HALO:, :])

    def inside(c):
        here = pl.ds(pl.multiple_of(c * BLOCK, BLOCK), BLOCK)
        cc = cm[here, :]
        low = slice(0, HALF)
        high = slice(HALF, BLOCK)
        at = pl.multiple_of(c * BLOCK, BLOCK)
        top = pl.ds(at, HALF)
        bottom = pl.ds(at + HALF, HALF)
        s_top = sc_keep[c, low, low]
        s_side = sc_keep[c, high, low]
        s_diag = sc_keep[c, high, high]
        causal = row_id[low, low] >= col_id[low, low]
        grown = widened(jnp.exp(drow_all[c]))
        for q in range(quads):
            span = slice(q * QUAD, (q + 1) * QUAD)
            xq = xc[here, span]
            tops = []
            bottoms = []
            parts = []
            for k in range(PER):
                h = q * PER + k
                d_top = dcol_all[top, h : h + 1]
                d_bottom = dcol_all[bottom, h : h + 1]
                e_low = e_keep[c, h : h + 1, low]
                e_high = e_keep[c, h : h + 1, high]
                tops.append((s_top * jnp.exp(jnp.where(causal, d_top - e_low, -jnp.inf))).astype(BF16))
                bottoms.append((s_side * jnp.exp(d_bottom - e_low)).astype(BF16))
                bottoms.append(
                    (s_diag * jnp.exp(jnp.where(causal, d_bottom - e_high, -jnp.inf))).astype(BF16)
                )
                mine = (lane >= k * HEADDIM) & (lane < (k + 1) * HEADDIM)
                parts.append(jnp.where(mine, xq, jnp.zeros_like(xq)))
            y_top = dot(
                jnp.concatenate(tops, axis=1),
                jnp.concatenate([part[low, :] for part in parts], axis=0),
            )
            y_bottom = dot(jnp.concatenate(bottoms, axis=1), jnp.concatenate(parts, axis=0))
            y = jnp.concatenate([y_top, y_bottom], axis=0)
            growth = dot(grown, expand[:, span])
            y = y + growth * dot(cc, ent[c, :, span])
            yl[here, span] = y + skrow[0:1, span] * xq.astype(F32)
            gr[here, span] = growth * jnp.exp(tl[c, 0:1, span])

    def gates(c):
        here = pl.ds(pl.multiple_of(c * BLOCK, BLOCK), BLOCK)
        normed = nrm[here, :]
        for q in range(quads):
            span = slice(q * QUAD, (q + 1) * QUAD)
            g = silu(dot(normed, wzx[:, span]))
            yl[here, span] = yl[here, span] * g
            gr[here, span] = gr[here, span] * g

    def state_copy(i):
        return remote(snd_s.at[i], got_s.at[i], cs.at[i], cr.at[i], mate, me)

    def advance(c, last):
        to_p(c).wait_recv()
        forwarded(c).wait_recv()
        here = pl.ds(pl.multiple_of(c * BLOCK, BLOCK), BLOCK)
        pieces = normalised(pl.ds(pl.multiple_of(HALO + c * BLOCK, HALO), BLOCK), BLOCK)
        for j in range(4):
            nrm[here, j * feat : (j + 1) * feat] = pieces[j]
        normed = nrm[here, :]
        bc = convolved(dot(normed, wbc[...]), slice(inner, inner + 2 * STATE), taps_bc[...])
        b = bc[:, :STATE].astype(BF16)
        cc = bc[:, STATE:].astype(BF16)
        cm[here, :] = cc
        raw_step = dot(normed, wdt[...]) + dtrow[0:1, :]
        step = jnp.maximum(raw_step, 0.0) + jnp.log1p(jnp.exp(-jnp.abs(raw_step)))
        srow = step.T[0:16, :]
        drow = drow_all[c]
        e_row = drow - jnp.log(srow)
        e_keep[c] = e_row
        wrow = jnp.exp(drow[:, BLOCK - 1 : BLOCK] - e_row)
        scores = lax.dot_general(cc, b, (((1,), (1,)), ((), ())), preferred_element_type=F32)
        sc_keep[c] = scores
        b_t = b.astype(F32).T.astype(BF16)
        weights = widened(wrow)
        for q in range(quads):
            span = slice(q * QUAD, (q + 1) * QUAD)
            raw = dot(normed, wzx[:, inner + q * QUAD : inner + (q + 1) * QUAD])
            xq = convolved(raw, span, taps_x[:, span]).astype(BF16)
            xc[here, span] = xq
            weighted = (xq.astype(F32) * dot(weights, expand[:, span])).astype(BF16)
            ent[c, :, span] = st[:, span].astype(BF16)
            now = et[c, 0:1, span] * st[:, span] + dot(b_t, weighted)
            st[:, span] = now
            if last:
                snd_s[q] = jnp.where(odd == 0, now[:, GROUP:], now[:, :GROUP]).astype(BF16)
                state_copy(q).start()

    def arrive(c):
        to_y(c).wait_recv()
        forward(c).start()

    def first(c, carry):
        advance(c, False)
        arrive(c + 1)

        inside(c)
        return carry

    arrive(0)
    lax.fori_loop(0, chunks - 1, first, 0)
    advance(chunks - 1, True)

    turns = inner // GROUP // 2

    def lanes_of(g):
        return pl.ds(pl.multiple_of(g * GROUP, GROUP), GROUP)

    def enter_copy(i):
        return remote(snd_e.at[i], got_e.at[i], es.at[i], er.at[i], ctx + 2, me)

    def leap_copy(i):
        return remote(snd_e.at[i], got_t.at[i], ts.at[i], tr.at[i], ctx + 4, me)

    def back_copy(i):
        return remote(snd_b.at[i], back.at[i], bs.at[i], br.at[i], mate, me)

    def pair_parts(i):
        at = lanes_of(2 * i + odd)
        mine, theirs = st[:, at], got_s[i].astype(F32)
        earlier = jnp.where(odd == 0, mine, theirs)
        later = jnp.where(odd == 0, theirs, mine)
        d_earlier = jnp.where(odd == 0, dsum[0:1, at], got_d[0:1, at])
        d_later = jnp.where(odd == 0, got_d[0:1, at], dsum[0:1, at])
        return at, earlier, later, d_earlier, d_later

    def hand_back(i, at, entered, earlier, d_earlier):
        after = jnp.exp(d_earlier) * entered + earlier
        snd_b[i] = jnp.where(odd == 0, after, entered).astype(BF16)
        inc[:, at] = jnp.where(odd == 0, entered, after).astype(BF16)
        back_copy(i).start()

    def relay_even():
        for i in range(turns):
            state_copy(i).wait_recv()
            at, earlier, later, d_earlier, d_later = pair_parts(i)

            @pl.when(ctx < places - 2)
            def _():
                snd_e[i] = (jnp.exp(d_later) * earlier + later).astype(BF16)
                enter_copy(i).start()

    def finish_even():
        for i in range(turns):

            @pl.when(pair > 0)
            def _():
                enter_copy(i).wait_recv()

            at, earlier, later, d_earlier, d_later = pair_parts(i)
            hand_back(i, at, got_e[i].astype(F32), earlier, d_earlier)

    def relay_odd():
        for i in range(turns):
            state_copy(i).wait_recv()
            enter_copy(i).wait_recv()
            at, earlier, later, d_earlier, d_later = pair_parts(i)

            @pl.when(pair > 1)
            def _():
                leap_copy(i).wait_recv()

            entered = jnp.exp(got_dp[0:1, at]) * got_t[i].astype(F32) + got_e[i].astype(F32)

            @pl.when(ctx < places - 2)
            def _():
                whole = jnp.exp(d_earlier + d_later) * entered + jnp.exp(d_later) * earlier + later
                snd_e[i] = whole.astype(BF16)
                enter_copy(i).start()

            @pl.when(ctx < places - 4)
            def _():
                leap_copy(i).start()

            hand_back(i, at, entered, earlier, d_earlier)

    @pl.when(ctx >= 2)
    def _():
        decay_pair_copy.wait_recv()

    @pl.when(ctx < 2)
    def _():
        got_e[...] = jnp.zeros_like(got_e)
        got_dp[...] = jnp.zeros_like(got_dp)

    @pl.when(pair <= 1)
    def _():
        got_t[...] = jnp.zeros_like(got_t)

    inside(chunks - 1)

    @pl.when(odd_pair == 0)
    def _():
        relay_even()

    half = chunks // 2

    def gate_step(c, carry):
        gates(c)
        return carry

    lax.fori_loop(0, half, gate_step, 0)

    @pl.when(pair == 1)
    def _():
        relay_odd()

    lax.fori_loop(half, chunks, gate_step, 0)

    @pl.when((odd_pair == 1) & (pair > 1))
    def _():
        relay_odd()

    @pl.when(odd_pair == 0)
    def _():
        finish_even()

    for load in out_loads:
        load.wait()

    for i in range(turns):
        back_copy(i).wait_recv()
        inc[:, lanes_of(2 * i + 1 - odd)] = back[i]

    def piece_copy(s):
        return remote(send_p.at[s], recv_p.at[s], rs.at[s], rr.at[s], ctx, partner)

    def far_copy(s):
        return remote(send_y.at[s], recv_y.at[s], zs.at[s], zr.at[s], ctx, other)

    def square_near(s):
        return remote(sq_own.at[s, pl.ds(0, 1)], sq_p.at[s, pl.ds(0, 1)], qs.at[0, s], qr.at[0, s], ctx, partner)

    def square_far(s):
        return remote(sq_sum.at[s, pl.ds(0, 1)], sq_far.at[s, pl.ds(0, 1)], qs.at[1, s], qr.at[1, s], ctx, other)

    def second(s, carry):
        here = pl.ds(pl.multiple_of(s * SUB, SUB), SUB)
        squares = jnp.zeros((SUB, 1), F32)
        cc = cm[here, :]
        for q in range(quads):
            span = slice(q * QUAD, (q + 1) * QUAD)
            gated = yl[here, span] + gr[here, span] * dot(cc, inc[:, span])
            squares = squares + jnp.sum(gated * gated, axis=-1, keepdims=True)
            gb[:, span] = (gated * out_gain[span].reshape(1, QUAD)).astype(BF16)
        g = gb[...]
        send_p[s] = dot(g, wout[:, 0 : 2 * feat]).astype(BF16)
        piece_copy(s).start()
        sq_own[s, 0:1, :] = jnp.broadcast_to(squares, (SUB, 128)).T[0:1, :]
        square_near(s).start()
        own[s] = dot(g, wout[:, 2 * feat : 4 * feat])
        piece_copy(s).wait_recv()
        send_y[s] = (own[s, :, 0:feat] + recv_p[s, :, feat : 2 * feat].astype(F32)).astype(BF16)
        far_copy(s).start()
        square_near(s).wait_recv()
        sq_sum[s, 0:1, :] = sq_own[s, 0:1, :] + sq_p[s, 0:1, :]
        square_far(s).start()
        own[s, :, feat : 2 * feat] = own[s, :, feat : 2 * feat] + recv_p[s, :, 0:feat].astype(F32)
        return carry

    lax.fori_loop(0, subs, second, 0)

    def third(s, carry):
        here = pl.ds(pl.multiple_of(s * SUB, SUB), SUB)
        square_far(s).wait_recv()
        scale_row = lax.rsqrt((sq_sum[s, 0:1, :] + sq_far[s, 0:1, :]) / (4 * inner) + eps)
        scale = jnp.broadcast_to(scale_row, (128, SUB)).T[:, 0:1]
        far_copy(s).wait_recv()
        out[here, :] = (
            (own[s, :, feat : 2 * feat] + recv_y[s].astype(F32)) * scale
        ).astype(BF16)
        return carry

    lax.fori_loop(0, subs, third, 0)

    for c in range(chunks):
        to_y(c).wait_send()
        to_p(c).wait_send()
        forward(c).wait_send()

    decay_copy.wait_send()
    for i in range(turns):
        state_copy(i).wait_send()
        back_copy(i).wait_send()

    @pl.when(ctx < places - 2)
    def _():
        decay_pair_copy.wait_send()
        for i in range(turns):
            enter_copy(i).wait_send()

    @pl.when((odd_pair == 1) & (ctx < places - 4))
    def _():
        for i in range(turns):
            leap_copy(i).wait_send()

    def drain(s, carry):
        piece_copy(s).wait_send()
        square_near(s).wait_send()
        far_copy(s).wait_send()
        square_far(s).wait_send()
        return carry

    lax.fori_loop(0, subs, drain, 0)

    @pl.when(ctx < places - 1)
    def _():
        for h in range(4):
            halo(h, me).wait_send()


def per_device(
    places,
    hidden,
    norm_gain,
    zx_weight,
    bc_weight,
    dt_weight,
    conv_x,
    conv_bc,
    dt_bias,
    log_decay,
    skip_gain,
    out_gain,
    out_weight,
):
    rows, feat = hidden.shape
    width = zx_weight.shape[0]
    inner = zx_weight.shape[2]
    turns = inner // GROUP // 2
    tiles = inner // LANES
    chunks = rows // BLOCK
    subs = rows // SUB
    any_spec = pl.BlockSpec(memory_space=pl.ANY)
    vmem = pl.BlockSpec(memory_space=pltpu.VMEM)
    smem = pl.BlockSpec(memory_space=pltpu.SMEM)
    dma = pltpu.SemaphoreType.DMA
    return pl.pallas_call(
        functools.partial(kernel, places),
        out_shape=jax.ShapeDtypeStruct((rows, feat), BF16),
        in_specs=[any_spec] * 4 + [vmem] * 4 + [smem, vmem, smem, vmem],
        out_specs=vmem,
        scratch_shapes=[
            pltpu.VMEM((4, HALO + rows, feat), BF16),
            pltpu.VMEM((tiles, width, 2, LANES), BF16),
            pltpu.VMEM((2, 2 * CUT, LANES), F32),
            pltpu.VMEM((width, 2 * inner), BF16),
            pltpu.VMEM((width, 2 * STATE), BF16),
            pltpu.VMEM((inner, width), BF16),
            pltpu.VMEM((width, 128), BF16),
            pltpu.VMEM((8, 128), F32),
            pltpu.VMEM((8, inner), F32),
            pltpu.VMEM((rows, width), BF16),
            pltpu.VMEM((HALO, inner + 2 * STATE), F32),
            pltpu.VMEM((16, BLOCK), F32),
            pltpu.VMEM((rows, inner), BF16),
            pltpu.VMEM((rows, STATE), BF16),
            pltpu.VMEM((rows, inner), F32),
            pltpu.VMEM((rows, inner), F32),
            pltpu.VMEM((chunks, STATE, inner), BF16),
            pltpu.VMEM((chunks, 8, inner), F32),
            pltpu.VMEM((chunks, 8, inner), F32),
            pltpu.VMEM((rows, 128), F32),
            pltpu.VMEM((128, inner), BF16),
            pltpu.VMEM((chunks, 16, BLOCK), F32),
            pltpu.VMEM((STATE, inner), F32),
            pltpu.VMEM((8, inner), F32),
            pltpu.VMEM((chunks, BLOCK, BLOCK), F32),
            pltpu.VMEM((chunks, 16, BLOCK), F32),
            pltpu.VMEM((8, inner), F32),
            pltpu.VMEM((8, inner), F32),
            pltpu.VMEM((8, inner), F32),
            pltpu.VMEM((turns, STATE, GROUP), BF16),
            pltpu.VMEM((turns, STATE, GROUP), BF16),
            pltpu.VMEM((turns, STATE, GROUP), BF16),
            pltpu.VMEM((turns, STATE, GROUP), BF16),
            pltpu.VMEM((turns, STATE, GROUP), BF16),
            pltpu.VMEM((turns, STATE, GROUP), BF16),
            pltpu.VMEM((turns, STATE, GROUP), BF16),
            pltpu.VMEM((STATE, inner), BF16),
            pltpu.VMEM((SUB, inner), BF16),
            pltpu.VMEM((subs, SUB, 2 * feat), BF16),
            pltpu.VMEM((subs, SUB, 2 * feat), BF16),
            pltpu.VMEM((subs, SUB, 2 * feat), F32),
            pltpu.VMEM((subs, SUB, feat), BF16),
            pltpu.VMEM((subs, SUB, feat), BF16),
            pltpu.VMEM((subs, 8, SUB), F32),
            pltpu.VMEM((subs, 8, SUB), F32),
            pltpu.VMEM((subs, 8, SUB), F32),
            pltpu.VMEM((subs, 8, SUB), F32),
            dma((6 + tiles,)),
            dma((chunks,)),
            dma((chunks,)),
            dma((chunks,)),
            dma((chunks,)),
            dma((chunks,)),
            dma((chunks,)),
            dma((4,)),
            dma((4,)),
            dma((2,)),
            dma((2,)),
            dma((turns,)),
            dma((turns,)),
            dma((turns,)),
            dma((turns,)),
            dma((turns,)),
            dma((turns,)),
            dma((turns,)),
            dma((turns,)),
            dma((subs,)),
            dma((subs,)),
            dma((subs,)),
            dma((subs,)),
            dma((2, subs)),
            dma((2, subs)),
        ],
        compiler_params=pltpu.CompilerParams(
            collective_id=0, has_side_effects=True, vmem_limit_bytes=63000000
        ),
        name="mixer",
    )(
        hidden,
        zx_weight,
        bc_weight,
        out_weight,
        norm_gain,
        dt_weight.T,
        conv_x,
        conv_bc,
        dt_bias,
        log_decay.T,
        skip_gain,
        out_gain,
    )


def solution(mesh):
    placed = (
        P("ctx", "head"),
        P(),
        P(None, None, "head"),
        P(),
        P(None, "head"),
        P(None, "head"),
        P(),
        P("head"),
        P("ctx", "head"),
        P("head"),
        P("head"),
        P("head", None),
    )
    return jax.shard_map(
        functools.partial(per_device, mesh.shape["ctx"]),
        mesh=mesh,
        in_specs=placed,
        out_specs=P("ctx", "head"),
        check_vma=False,
    )
```

```python
import functools

import jax
import jax.numpy as jnp
from jax import lax
from jax.experimental import pallas as pl
from jax.experimental.pallas import tpu as pltpu
from jax.sharding import PartitionSpec as P

HEADDIM = 64
STATE = 128
CONV = 4
BLOCK = 256
HALO = 16
QUAD = 256
GROUP = 128
PER = QUAD // HEADDIM
SUB = 128
HALF = BLOCK // 2
LANES = 128
CUT = 256

eps = 1e-05
F32 = jnp.float32
BF16 = jnp.bfloat16


def dot(a, b):
    return jnp.dot(a, b, preferred_element_type=F32)


def silu(v):
    half = 0.5 * v
    return half + half * jnp.tanh(half)


def spread(column_of, first, lane, rows):
    out = None
    for k in range(PER):
        piece = jnp.broadcast_to(column_of(first + k), (rows, QUAD))
        out = piece if out is None else jnp.where(lane >= k * HEADDIM, piece, out)
    return out


def kernel(
    places,
    hidden,
    wzx_hbm,
    wbc_hbm,
    wout_hbm,
    gain,
    wdt_in,
    taps_x,
    taps_bc,
    dtb,
    ld_in,
    skip,
    out_gain,
    out,
    xg,
    wraw,
    wf,
    wzx,
    wbc,
    wout,
    wdt,
    dtrow,
    skrow,
    nrm,
    tail,
    ldp,
    xc,
    cm,
    yl,
    gr,
    ent,
    tl,
    et,
    dcol_all,
    expand,
    drow_all,
    st,
    dsum,
    bm,
    e_keep,
    got_d,
    dpair,
    got_dp,
    got_s,
    snd_s,
    got_e,
    got_t,
    snd_e,
    snd_b,
    back,
    inc,
    gb,
    send_p,
    recv_p,
    own,
    held,
    ready,
    send_y,
    recv_y,
    sq_own,
    sq_p,
    sq_sum,
    sq_far,
    load_sem,
    ys,
    yr,
    ps,
    pr,
    fs,
    fr,
    hs,
    hr,
    ds_,
    dr_,
    cs,
    cr,
    es,
    er,
    ts,
    tr,
    bs,
    br,
    rs,
    rr,
    zs,
    zr,
    qs,
    qr,
    out_sem,
):
    rows, feat = hidden.shape
    width = 4 * feat
    inner = wzx.shape[1] // 2
    heads = inner // HEADDIM
    quads = inner // QUAD
    chunks = rows // BLOCK
    subs = rows // SUB
    tiles = inner // LANES
    ctx = lax.axis_index("ctx")
    me = lax.axis_index("head")
    partner = me + 1 - 2 * lax.rem(me, 2)
    other = lax.rem(me + 2, 4)
    diag = lax.rem(partner + 2, 4)
    odd = lax.rem(ctx, 2)
    mate = ctx + 1 - 2 * odd
    pair = lax.div(ctx, 2)
    odd_pair = lax.rem(pair, 2)
    MESH = pl.DeviceIdType.MESH

    def remote(src, dst, ss, rsem, c, h):
        return pltpu.make_async_remote_copy(
            src_ref=src, dst_ref=dst, send_sem=ss, recv_sem=rsem, device_id=(c, h), device_id_type=MESH
        )

    def columns(h):
        return pl.ds(pl.multiple_of(h * feat, 128), feat)

    own_load = pltpu.make_async_copy(hidden, xg.at[me, pl.ds(HALO, rows)], load_sem.at[0])
    bc_load = pltpu.make_async_copy(wbc_hbm, wbc, load_sem.at[1])
    zx_loads = [
        pltpu.make_async_copy(
            wzx_hbm.at[:, :, pl.ds(j * LANES, LANES)], wraw.at[j], load_sem.at[6 + j]
        )
        for j in range(tiles)
    ]
    out_loads = [
        pltpu.make_async_copy(
            wout_hbm.at[:, columns(h)], wout.at[:, pl.ds(k * feat, feat)], load_sem.at[2 + k]
        )
        for k, h in enumerate((diag, other, partner, me))
    ]

    barrier = pltpu.get_barrier_semaphore()

    def greet(c, h):
        pl.semaphore_signal(barrier, inc=1, device_id=(c, h), device_id_type=MESH)

    for h in (partner, other, diag):
        greet(ctx, h)

    @pl.when(ctx > 0)
    def _():
        for h in range(4):
            greet(ctx - 1, h)

    @pl.when(ctx < places - 1)
    def _():
        for h in range(4):
            greet(ctx + 1, h)

    for gap in (2, 4):

        @pl.when(ctx >= gap)
        def _():
            greet(ctx - gap, me)

        @pl.when(ctx < places - gap)
        def _():
            greet(ctx + gap, me)

    own_load.start()
    for load in zx_loads:
        load.start()
    bc_load.start()
    for load in out_loads:
        load.start()

    lane = lax.broadcasted_iota(jnp.int32, (1, QUAD), 1)
    row_id = lax.broadcasted_iota(jnp.int32, (BLOCK, BLOCK), 0)
    col_id = lax.broadcasted_iota(jnp.int32, (BLOCK, BLOCK), 1)

    def widened(per_head):
        high = per_head.astype(BF16).astype(F32)
        stack = jnp.concatenate([high, per_head - high, jnp.zeros((96, BLOCK), F32)], axis=0)
        return stack.T.astype(BF16)

    def split(j):
        flat = wraw.at[j].reshape(2 * width, LANES)

        def step(i, carry):
            for u in range(2):
                at = pl.multiple_of((2 * i + u) * CUT, CUT)
                wf[u] = flat[pl.ds(pl.multiple_of(2 * at, 2 * CUT), 2 * CUT), :].astype(F32)
                for g in range(2):
                    first = g * inner + j * LANES
                    wzx[pl.ds(at, CUT), first : first + LANES] = wf[
                        u, pl.ds(g, CUT, stride=2), :
                    ].astype(BF16)
            return carry

        lax.fori_loop(0, width // (2 * CUT), step, 0)

    dt_wide = jnp.concatenate(
        [wdt_in[...].astype(F32), jnp.zeros((128 - heads, width), F32)], axis=0
    )
    wdt[...] = dt_wide.T.astype(BF16)
    few = lax.broadcasted_iota(jnp.int32, (8, 128), 1)
    bias_row = jnp.zeros((8, 128), F32)
    for h in range(heads):
        bias_row = jnp.where(few == h, dtb[h], bias_row)
    dtrow[...] = bias_row
    wide = lax.broadcasted_iota(jnp.int32, (8, inner), 1)
    skip_row = jnp.zeros((8, inner), F32)
    for h in range(heads):
        skip_row = jnp.where(wide >= h * HEADDIM, skip[h], skip_row)
    skrow[...] = skip_row
    which = lax.broadcasted_iota(jnp.int32, (128, inner), 0)
    which = jnp.where(which >= 16, which - 16, which)
    across = lax.broadcasted_iota(jnp.int32, (128, inner), 1)
    within = (across >= which * HEADDIM) & (across < (which + 1) * HEADDIM)
    expand[...] = jnp.where(within, 1.0, 0.0).astype(BF16)
    st[...] = jnp.zeros_like(st)
    dsum[...] = jnp.zeros_like(dsum)
    ldp[...] = jnp.zeros_like(ldp)
    tri = jnp.where(row_id <= col_id, 1.0, 0.0).astype(F32)

    def decays(c, carry):
        here = pl.ds(pl.multiple_of(c * BLOCK, BLOCK), BLOCK)
        ldp[0:heads, :] = ld_in[:, here]
        drow = jnp.dot(ldp[...], tri, preferred_element_type=F32, precision=lax.Precision.HIGHEST)
        dcol = jnp.concatenate([drow, jnp.zeros((112, BLOCK), F32)], axis=0).T
        drow_all[c] = drow
        dcol_all[here, :] = dcol
        tl[c] = dsum[...]
        for q in range(quads):
            span = slice(q * QUAD, (q + 1) * QUAD)
            total = spread(lambda i: dcol[BLOCK - 1 : BLOCK, i : i + 1], q * PER, lane, 1)
            et[c, :, span] = jnp.broadcast_to(jnp.exp(total), (8, QUAD))
            dsum[:, span] = dsum[:, span] + total
        return carry

    lax.fori_loop(0, chunks, decays, 0)

    below = lax.div(ctx + places - 1, places)
    above = lax.div(2 * places - 2 - ctx, places)
    hops = 0
    for gap in (2, 4):
        hops = hops + lax.div(ctx + places - gap, places)
        hops = hops + lax.div(2 * places - 1 - gap - ctx, places)
    pl.semaphore_wait(barrier, 3 + 4 * (below + above) + hops)

    def src_rows(c):
        return hidden.at[pl.ds(pl.multiple_of(c * BLOCK, BLOCK), BLOCK)]

    def slot(h, c):
        return xg.at[h, pl.ds(pl.multiple_of(HALO + c * BLOCK, HALO), BLOCK)]

    def to_y(c):
        return remote(src_rows(c), slot(me, c), ys.at[c], yr.at[c], ctx, other)

    def to_p(c):
        return remote(src_rows(c), slot(me, c), ps.at[c], pr.at[c], ctx, partner)

    def forward(c):
        return remote(slot(other, c), slot(other, c), fs.at[c], fr.at[c], ctx, partner)

    def forwarded(c):
        return remote(slot(diag, c), slot(diag, c), fs.at[c], fr.at[c], ctx, partner)

    def halo(h, sender):
        return remote(
            hidden.at[pl.ds(rows - HALO, HALO)],
            xg.at[sender, pl.ds(0, HALO)],
            hs.at[h],
            hr.at[sender],
            ctx + 1,
            h,
        )

    decay_copy = remote(dsum, got_d, ds_.at[0], dr_.at[0], mate, me)
    decay_pair_copy = remote(dpair, got_dp, ds_.at[1], dr_.at[1], ctx + 2, me)

    @pl.when(ctx < places - 1)
    def _():
        for h in range(4):
            halo(h, me).start()

    for c in range(chunks):
        to_y(c).start()
    for c in range(chunks):
        to_p(c).start()

    @pl.when(ctx == 0)
    def _():
        xg[:, 0:HALO, :] = jnp.zeros((4, HALO, feat), BF16)

    decay_copy.start()

    for j in range(tiles):
        zx_loads[j].wait()
        split(j)

    bc_load.wait()
    own_load.wait()
    decay_copy.wait_recv()
    dpair[...] = dsum[...] + got_d[...]

    @pl.when(ctx < places - 2)
    def _():
        decay_pair_copy.start()

    @pl.when(ctx > 0)
    def _():
        for h in range(4):
            halo(0, h).wait_recv()

    def normalised(at, count):
        vals = [xg[j, at, :].astype(F32) for j in range(4)]
        total = sum(jnp.sum(v * v, axis=-1, keepdims=True) for v in vals)
        scale = lax.rsqrt(total / width + eps)
        return [
            (vals[j] * scale * gain[j * feat : (j + 1) * feat].reshape(1, feat)).astype(BF16)
            for j in range(4)
        ]

    head_rows = jnp.concatenate(normalised(pl.ds(0, HALO), HALO), axis=1)
    for s in range(quads):
        tail[:, s * QUAD : (s + 1) * QUAD] = dot(
            head_rows, wzx[:, inner + s * QUAD : inner + (s + 1) * QUAD]
        )
    tail[:, inner : inner + 2 * STATE] = dot(head_rows, wbc[...])

    def convolved(raw, span, taps):
        ext = jnp.concatenate([tail[:, span], raw], axis=0)
        summed = taps[CONV : CONV + 1, :] + taps[CONV - 1 : CONV, :] * ext
        for back_by in range(1, CONV):
            at = CONV - 1 - back_by
            summed = summed + taps[at : at + 1, :] * pltpu.roll(ext, back_by, 0)
        tail[:, span] = raw[BLOCK - HALO :, :]
        return silu(summed[HALO:, :])

    def inside(c):
        here = pl.ds(pl.multiple_of(c * BLOCK, BLOCK), BLOCK)
        cc = cm[here, :]
        low = slice(0, HALF)
        high = slice(HALF, BLOCK)
        at = pl.multiple_of(c * BLOCK, BLOCK)
        top = pl.ds(at, HALF)
        bottom = pl.ds(at + HALF, HALF)
        scores = lax.dot_general(
            cc, bm[here, :], (((1,), (1,)), ((), ())), preferred_element_type=F32
        )
        s_top = scores[low, low]
        s_side = scores[high, low]
        s_diag = scores[high, high]
        causal = row_id[low, low] >= col_id[low, low]
        grown = widened(jnp.exp(drow_all[c]))
        for q in range(quads):
            span = slice(q * QUAD, (q + 1) * QUAD)
            xq = xc[here, span]
            tops = []
            bottoms = []
            parts = []
            for k in range(PER):
                h = q * PER + k
                d_top = dcol_all[top, h : h + 1]
                d_bottom = dcol_all[bottom, h : h + 1]
                e_low = e_keep[c, h : h + 1, low]
                e_high = e_keep[c, h : h + 1, high]
                tops.append((s_top * jnp.exp(jnp.where(causal, d_top - e_low, -jnp.inf))).astype(BF16))
                bottoms.append((s_side * jnp.exp(d_bottom - e_low)).astype(BF16))
                bottoms.append(
                    (s_diag * jnp.exp(jnp.where(causal, d_bottom - e_high, -jnp.inf))).astype(BF16)
                )
                mine = (lane >= k * HEADDIM) & (lane < (k + 1) * HEADDIM)
                parts.append(jnp.where(mine, xq, jnp.zeros_like(xq)))
            y_top = dot(
                jnp.concatenate(tops, axis=1),
                jnp.concatenate([part[low, :] for part in parts], axis=0),
            )
            y_bottom = dot(jnp.concatenate(bottoms, axis=1), jnp.concatenate(parts, axis=0))
            y = jnp.concatenate([y_top, y_bottom], axis=0)
            growth = dot(grown, expand[:, span])
            y = y + growth * dot(cc, ent[c, :, span])
            yl[here, span] = y + skrow[0:1, span] * xq.astype(F32)
            gr[here, span] = growth * jnp.exp(tl[c, 0:1, span])

    def gates(c):
        here = pl.ds(pl.multiple_of(c * BLOCK, BLOCK), BLOCK)
        opened = silu(dot(nrm[here, :], wzx[:, 0:inner]))
        for q in range(quads):
            span = slice(q * QUAD, (q + 1) * QUAD)
            g = opened[:, span]
            yl[here, span] = yl[here, span] * g
            gr[here, span] = gr[here, span] * g

    def state_copy(i):
        return remote(snd_s.at[i], got_s.at[i], cs.at[i], cr.at[i], mate, me)

    def advance(c, last):
        to_p(c).wait_recv()
        forwarded(c).wait_recv()
        here = pl.ds(pl.multiple_of(c * BLOCK, BLOCK), BLOCK)
        pieces = normalised(pl.ds(pl.multiple_of(HALO + c * BLOCK, HALO), BLOCK), BLOCK)
        for j in range(4):
            nrm[here, j * feat : (j + 1) * feat] = pieces[j]
        normed = nrm[here, :]
        bc = convolved(dot(normed, wbc[...]), slice(inner, inner + 2 * STATE), taps_bc[...])
        b = bc[:, :STATE].astype(BF16)
        cc = bc[:, STATE:].astype(BF16)
        cm[here, :] = cc
        raw_step = dot(normed, wdt[...]) + dtrow[0:1, :]
        step = jnp.maximum(raw_step, 0.0) + jnp.log1p(jnp.exp(-jnp.abs(raw_step)))
        srow = step.T[0:16, :]
        drow = drow_all[c]
        e_row = drow - jnp.log(srow)
        e_keep[c] = e_row
        wrow = jnp.exp(drow[:, BLOCK - 1 : BLOCK] - e_row)
        bm[here, :] = b
        b_t = b.astype(F32).T.astype(BF16)
        weights = widened(wrow)
        raws = dot(normed, wzx[:, inner : 2 * inner])
        for q in range(quads):
            span = slice(q * QUAD, (q + 1) * QUAD)
            raw = raws[:, span]
            xq = convolved(raw, span, taps_x[:, span]).astype(BF16)
            xc[here, span] = xq
            weighted = (xq.astype(F32) * dot(weights, expand[:, span])).astype(BF16)
            ent[c, :, span] = st[:, span].astype(BF16)
            now = et[c, 0:1, span] * st[:, span] + dot(b_t, weighted)
            st[:, span] = now
            if last:
                snd_s[q] = jnp.where(odd == 0, now[:, GROUP:], now[:, :GROUP]).astype(BF16)
                state_copy(q).start()

    def arrive(c):
        to_y(c).wait_recv()
        forward(c).start()

    def first(c, carry):
        advance(c, False)
        arrive(c + 1)

        @pl.when(pair > 0)
        def _():
            inside(c)

        return carry

    arrive(0)
    lax.fori_loop(0, chunks - 1, first, 0)
    advance(chunks - 1, True)

    turns = inner // GROUP // 2

    def lanes_of(g):
        return pl.ds(pl.multiple_of(g * GROUP, GROUP), GROUP)

    def enter_copy(i):
        return remote(snd_e.at[i], got_e.at[i], es.at[i], er.at[i], ctx + 2, me)

    def leap_copy(i):
        return remote(snd_e.at[i], got_t.at[i], ts.at[i], tr.at[i], ctx + 4, me)

    def back_copy(i):
        return remote(snd_b.at[i], back.at[i], bs.at[i], br.at[i], mate, me)

    def pair_parts(i):
        at = lanes_of(2 * i + odd)
        mine, theirs = st[:, at], got_s[i].astype(F32)
        earlier = jnp.where(odd == 0, mine, theirs)
        later = jnp.where(odd == 0, theirs, mine)
        d_earlier = jnp.where(odd == 0, dsum[0:1, at], got_d[0:1, at])
        d_later = jnp.where(odd == 0, got_d[0:1, at], dsum[0:1, at])
        return at, earlier, later, d_earlier, d_later

    def hand_back(i, at, entered, earlier, d_earlier):
        after = jnp.exp(d_earlier) * entered + earlier
        snd_b[i] = jnp.where(odd == 0, after, entered).astype(BF16)
        inc[:, at] = jnp.where(odd == 0, entered, after).astype(BF16)
        back_copy(i).start()

    def relay_even():
        for i in range(turns):
            state_copy(i).wait_recv()
            at, earlier, later, d_earlier, d_later = pair_parts(i)

            @pl.when(ctx < places - 2)
            def _():
                snd_e[i] = (jnp.exp(d_later) * earlier + later).astype(BF16)
                enter_copy(i).start()

    def finish_even():
        for i in range(turns):

            @pl.when(pair > 0)
            def _():
                enter_copy(i).wait_recv()

            at, earlier, later, d_earlier, d_later = pair_parts(i)
            hand_back(i, at, got_e[i].astype(F32), earlier, d_earlier)

    def relay_odd():
        for i in range(turns):
            state_copy(i).wait_recv()
            enter_copy(i).wait_recv()
            at, earlier, later, d_earlier, d_later = pair_parts(i)

            @pl.when(pair > 1)
            def _():
                leap_copy(i).wait_recv()

            entered = jnp.exp(got_dp[0:1, at]) * got_t[i].astype(F32) + got_e[i].astype(F32)

            @pl.when(ctx < places - 2)
            def _():
                whole = jnp.exp(d_earlier + d_later) * entered + jnp.exp(d_later) * earlier + later
                snd_e[i] = whole.astype(BF16)

                @pl.when(ctx < places - 4)
                def _():
                    leap_copy(i).start()

                enter_copy(i).start()

            hand_back(i, at, entered, earlier, d_earlier)

    @pl.when(ctx >= 2)
    def _():
        decay_pair_copy.wait_recv()

    @pl.when(ctx < 2)
    def _():
        got_e[...] = jnp.zeros_like(got_e)
        got_dp[...] = jnp.zeros_like(got_dp)

    @pl.when(pair <= 1)
    def _():
        got_t[...] = jnp.zeros_like(got_t)

    inside(chunks - 1)

    @pl.when(odd_pair == 0)
    def _():
        relay_even()

    @pl.when(pair == 0)
    def _():
        finish_even()

    half = chunks // 2

    def gate_step(c, carry):
        gates(c)
        return carry

    @pl.when(pair > 0)
    def _():
        lax.fori_loop(0, half, gate_step, 0)

    @pl.when(pair == 1)
    def _():
        relay_odd()

    @pl.when(pair > 0)
    def _():
        lax.fori_loop(half, chunks, gate_step, 0)

    @pl.when((odd_pair == 1) & (pair > 1))
    def _():
        relay_odd()

    @pl.when((odd_pair == 0) & (pair > 0))
    def _():
        finish_even()

    for load in out_loads:
        load.wait()

    for i in range(turns):
        back_copy(i).wait_recv()
        inc[:, lanes_of(2 * i + 1 - odd)] = back[i]

    def piece_copy(k, s):
        return remote(send_p.at[k, s], recv_p.at[k, s], rs.at[k, s], rr.at[k, s], ctx, partner)

    def far_copy(s):
        return remote(send_y.at[s], recv_y.at[s], zs.at[s], zr.at[s], ctx, other)

    def square_near(s):
        return remote(sq_own.at[s, pl.ds(0, 1)], sq_p.at[s, pl.ds(0, 1)], qs.at[0, s], qr.at[0, s], ctx, partner)

    def square_far(s):
        return remote(sq_sum.at[s, pl.ds(0, 1)], sq_far.at[s, pl.ds(0, 1)], qs.at[1, s], qr.at[1, s], ctx, other)

    def combine(s):
        piece_copy(0, s).wait_recv()
        send_y[s] = (held[s] + recv_p[0, s].astype(F32)).astype(BF16)
        far_copy(s).start()
        square_near(s).wait_recv()
        sq_sum[s, 0:1, :] = sq_own[s, 0:1, :] + sq_p[s, 0:1, :]
        square_far(s).start()

    def second(s, carry):
        @pl.when((pair == 0) & (lax.rem(s, BLOCK // SUB) == 0))
        def _():
            c = lax.div(s, BLOCK // SUB)

            @pl.when(c < chunks - 1)
            def _():
                inside(c)

            gates(c)

        here = pl.ds(pl.multiple_of(s * SUB, SUB), SUB)
        squares = jnp.zeros((SUB, 1), F32)
        cc = cm[here, :]
        for q in range(quads):
            span = slice(q * QUAD, (q + 1) * QUAD)
            gated = yl[here, span] + gr[here, span] * dot(cc, inc[:, span])
            squares = squares + jnp.sum(gated * gated, axis=-1, keepdims=True)
            gb[:, span] = (gated * out_gain[span].reshape(1, QUAD)).astype(BF16)
        g = gb[...]
        across = dot(g, wout[:, 0 : 2 * feat])
        send_p[0, s] = across[:, 0:feat].astype(BF16)
        piece_copy(0, s).start()
        sq_own[s, 0:1, :] = jnp.broadcast_to(squares, (SUB, 128)).T[0:1, :]
        square_near(s).start()
        staying = dot(g, wout[:, 2 * feat : 4 * feat])
        send_p[1, s] = staying[:, 0:feat].astype(BF16)
        piece_copy(1, s).start()
        own[s] = staying[:, feat : 2 * feat]
        held[s] = across[:, feat : 2 * feat]

        @pl.when(s == 0)
        def _():
            combine(s)

        @pl.when(s > 1)
        def _():
            combine(s - 1)

        return carry

    lax.fori_loop(0, subs, second, 0)
    combine(subs - 1)

    def leave(s):
        here = pl.ds(pl.multiple_of(s * SUB, SUB), SUB)
        return pltpu.make_async_copy(ready.at[here], out.at[here], out_sem.at[s])

    def third(s, carry):
        here = pl.ds(pl.multiple_of(s * SUB, SUB), SUB)
        piece_copy(1, s).wait_recv()
        mine = own[s] + recv_p[1, s].astype(F32)
        square_far(s).wait_recv()
        scale_row = lax.rsqrt((sq_sum[s, 0:1, :] + sq_far[s, 0:1, :]) / (4 * inner) + eps)
        scale = jnp.broadcast_to(scale_row, (128, SUB)).T[:, 0:1]
        far_copy(s).wait_recv()
        ready[here, :] = ((mine + recv_y[s].astype(F32)) * scale).astype(BF16)
        leave(s).start()
        return carry

    lax.fori_loop(0, subs, third, 0)

    for c in range(chunks):
        to_y(c).wait_send()
        to_p(c).wait_send()
        forward(c).wait_send()

    decay_copy.wait_send()
    for i in range(turns):
        state_copy(i).wait_send()
        back_copy(i).wait_send()

    @pl.when(ctx < places - 2)
    def _():
        decay_pair_copy.wait_send()
        for i in range(turns):
            enter_copy(i).wait_send()

    @pl.when((odd_pair == 1) & (ctx < places - 4))
    def _():
        for i in range(turns):
            leap_copy(i).wait_send()

    def drain(s, carry):
        piece_copy(0, s).wait_send()
        piece_copy(1, s).wait_send()
        leave(s).wait()
        square_near(s).wait_send()
        far_copy(s).wait_send()
        square_far(s).wait_send()
        return carry

    lax.fori_loop(0, subs, drain, 0)

    @pl.when(ctx < places - 1)
    def _():
        for h in range(4):
            halo(h, me).wait_send()


def per_device(
    places,
    hidden,
    norm_gain,
    zx_weight,
    bc_weight,
    dt_weight,
    conv_x,
    conv_bc,
    dt_bias,
    log_decay,
    skip_gain,
    out_gain,
    out_weight,
):
    rows, feat = hidden.shape
    width = zx_weight.shape[0]
    inner = zx_weight.shape[2]
    turns = inner // GROUP // 2
    tiles = inner // LANES
    chunks = rows // BLOCK
    subs = rows // SUB
    any_spec = pl.BlockSpec(memory_space=pl.ANY)
    vmem = pl.BlockSpec(memory_space=pltpu.VMEM)
    smem = pl.BlockSpec(memory_space=pltpu.SMEM)
    dma = pltpu.SemaphoreType.DMA
    return pl.pallas_call(
        functools.partial(kernel, places),
        out_shape=jax.ShapeDtypeStruct((rows, feat), BF16),
        in_specs=[any_spec] * 4 + [vmem] * 4 + [smem, vmem, smem, vmem],
        out_specs=any_spec,
        scratch_shapes=[
            pltpu.VMEM((4, HALO + rows, feat), BF16),
            pltpu.VMEM((tiles, width, 2, LANES), BF16),
            pltpu.VMEM((2, 2 * CUT, LANES), F32),
            pltpu.VMEM((width, 2 * inner), BF16),
            pltpu.VMEM((width, 2 * STATE), BF16),
            pltpu.VMEM((inner, width), BF16),
            pltpu.VMEM((width, 128), BF16),
            pltpu.VMEM((8, 128), F32),
            pltpu.VMEM((8, inner), F32),
            pltpu.VMEM((rows, width), BF16),
            pltpu.VMEM((HALO, inner + 2 * STATE), F32),
            pltpu.VMEM((16, BLOCK), F32),
            pltpu.VMEM((rows, inner), BF16),
            pltpu.VMEM((rows, STATE), BF16),
            pltpu.VMEM((rows, inner), F32),
            pltpu.VMEM((rows, inner), F32),
            pltpu.VMEM((chunks, STATE, inner), BF16),
            pltpu.VMEM((chunks, 8, inner), F32),
            pltpu.VMEM((chunks, 8, inner), F32),
            pltpu.VMEM((rows, 128), F32),
            pltpu.VMEM((128, inner), BF16),
            pltpu.VMEM((chunks, 16, BLOCK), F32),
            pltpu.VMEM((STATE, inner), F32),
            pltpu.VMEM((8, inner), F32),
            pltpu.VMEM((rows, STATE), BF16),
            pltpu.VMEM((chunks, 16, BLOCK), F32),
            pltpu.VMEM((8, inner), F32),
            pltpu.VMEM((8, inner), F32),
            pltpu.VMEM((8, inner), F32),
            pltpu.VMEM((turns, STATE, GROUP), BF16),
            pltpu.VMEM((turns, STATE, GROUP), BF16),
            pltpu.VMEM((turns, STATE, GROUP), BF16),
            pltpu.VMEM((turns, STATE, GROUP), BF16),
            pltpu.VMEM((turns, STATE, GROUP), BF16),
            pltpu.VMEM((turns, STATE, GROUP), BF16),
            pltpu.VMEM((turns, STATE, GROUP), BF16),
            pltpu.VMEM((STATE, inner), BF16),
            pltpu.VMEM((SUB, inner), BF16),
            pltpu.VMEM((2, subs, SUB, feat), BF16),
            pltpu.VMEM((2, subs, SUB, feat), BF16),
            pltpu.VMEM((subs, SUB, feat), F32),
            pltpu.VMEM((subs, SUB, feat), F32),
            pltpu.VMEM((rows, feat), BF16),
            pltpu.VMEM((subs, SUB, feat), BF16),
            pltpu.VMEM((subs, SUB, feat), BF16),
            pltpu.VMEM((subs, 8, SUB), F32),
            pltpu.VMEM((subs, 8, SUB), F32),
            pltpu.VMEM((subs, 8, SUB), F32),
            pltpu.VMEM((subs, 8, SUB), F32),
            dma((6 + tiles,)),
            dma((chunks,)),
            dma((chunks,)),
            dma((chunks,)),
            dma((chunks,)),
            dma((chunks,)),
            dma((chunks,)),
            dma((4,)),
            dma((4,)),
            dma((2,)),
            dma((2,)),
            dma((turns,)),
            dma((turns,)),
            dma((turns,)),
            dma((turns,)),
            dma((turns,)),
            dma((turns,)),
            dma((turns,)),
            dma((turns,)),
            dma((2, subs)),
            dma((2, subs)),
            dma((subs,)),
            dma((subs,)),
            dma((2, subs)),
            dma((2, subs)),
            dma((subs,)),
        ],
        compiler_params=pltpu.CompilerParams(
            collective_id=0, has_side_effects=True, vmem_limit_bytes=63000000
        ),
        name="mixer",
    )(
        hidden,
        zx_weight,
        bc_weight,
        out_weight,
        norm_gain,
        dt_weight.T,
        conv_x,
        conv_bc,
        dt_bias,
        log_decay.T,
        skip_gain,
        out_gain,
    )


def solution(mesh):
    placed = (
        P("ctx", "head"),
        P(),
        P(None, None, "head"),
        P(),
        P(None, "head"),
        P(None, "head"),
        P(),
        P("head"),
        P("ctx", "head"),
        P("head"),
        P("head"),
        P("head", None),
    )
    return jax.shard_map(
        functools.partial(per_device, mesh.shape["ctx"]),
        mesh=mesh,
        in_specs=placed,
        out_specs=P("ctx", "head"),
        check_vma=False,
    )
```

```python
import functools

import jax
import jax.numpy as jnp
from jax import lax
from jax.experimental import pallas as pl
from jax.experimental.pallas import tpu as pltpu
from jax.sharding import PartitionSpec as P

HEADDIM = 64
STATE = 128
CONV = 4
BLOCK = 256
HALO = 16
QUAD = 256
GROUP = 128
PER = QUAD // HEADDIM
SUB = 128
HALF = BLOCK // 2
LANES = 128
CUT = 256

eps = 1e-05
F32 = jnp.float32
BF16 = jnp.bfloat16


def dot(a, b):
    return jnp.dot(a, b, preferred_element_type=F32)


def silu(v):
    half = 0.5 * v
    return half + half * jnp.tanh(half)


def spread(column_of, first, lane, rows):
    out = None
    for k in range(PER):
        piece = jnp.broadcast_to(column_of(first + k), (rows, QUAD))
        out = piece if out is None else jnp.where(lane >= k * HEADDIM, piece, out)
    return out


def kernel(
    places,
    hidden,
    wzx_hbm,
    wbc_hbm,
    wout_hbm,
    gain,
    wdt_in,
    taps_x,
    taps_bc,
    dtb,
    ld_in,
    skip,
    out_gain,
    out,
    xg,
    wraw,
    wf,
    wzx,
    wbc,
    wout,
    wdt,
    dtrow,
    skrow,
    nrm,
    tail,
    ldp,
    xc,
    cm,
    yl,
    gr,
    ent,
    tl,
    et,
    dcol_all,
    expand,
    drow_all,
    st,
    dsum,
    bm,
    e_keep,
    got_d,
    dpair,
    got_dp,
    got_s,
    snd_s,
    got_e,
    got_t,
    snd_e,
    snd_b,
    back,
    inc,
    gb,
    send_p,
    recv_p,
    own,
    held,
    ready,
    send_y,
    recv_y,
    sq_own,
    sq_p,
    sq_sum,
    sq_far,
    load_sem,
    ys,
    yr,
    ps,
    pr,
    fs,
    fr,
    hs,
    hr,
    ds_,
    dr_,
    cs,
    cr,
    es,
    er,
    ts,
    tr,
    bs,
    br,
    rs,
    rr,
    zs,
    zr,
    qs,
    qr,
    out_sem,
):
    rows, feat = hidden.shape
    width = 4 * feat
    inner = wzx.shape[1] // 2
    heads = inner // HEADDIM
    quads = inner // QUAD
    chunks = rows // BLOCK
    subs = rows // SUB
    tiles = inner // LANES
    ctx = lax.axis_index("ctx")
    me = lax.axis_index("head")
    partner = me + 1 - 2 * lax.rem(me, 2)
    other = lax.rem(me + 2, 4)
    diag = lax.rem(partner + 2, 4)
    odd = lax.rem(ctx, 2)
    mate = ctx + 1 - 2 * odd
    pair = lax.div(ctx, 2)
    odd_pair = lax.rem(pair, 2)
    MESH = pl.DeviceIdType.MESH

    def remote(src, dst, ss, rsem, c, h):
        return pltpu.make_async_remote_copy(
            src_ref=src, dst_ref=dst, send_sem=ss, recv_sem=rsem, device_id=(c, h), device_id_type=MESH
        )

    def columns(h):
        return pl.ds(pl.multiple_of(h * feat, 128), feat)

    own_load = pltpu.make_async_copy(hidden, xg.at[me, pl.ds(HALO, rows)], load_sem.at[0])
    bc_load = pltpu.make_async_copy(wbc_hbm, wbc, load_sem.at[1])
    zx_loads = [
        pltpu.make_async_copy(
            wzx_hbm.at[:, :, pl.ds(j * LANES, LANES)], wraw.at[j], load_sem.at[6 + j]
        )
        for j in range(tiles)
    ]
    out_loads = [
        pltpu.make_async_copy(
            wout_hbm.at[:, columns(h)], wout.at[:, pl.ds(k * feat, feat)], load_sem.at[2 + k]
        )
        for k, h in enumerate((diag, other, partner, me))
    ]

    barrier = pltpu.get_barrier_semaphore()

    def greet(c, h):
        pl.semaphore_signal(barrier, inc=1, device_id=(c, h), device_id_type=MESH)

    for h in (partner, other, diag):
        greet(ctx, h)

    @pl.when(ctx > 0)
    def _():
        for h in range(4):
            greet(ctx - 1, h)

    @pl.when(ctx < places - 1)
    def _():
        for h in range(4):
            greet(ctx + 1, h)

    for gap in (2, 4):

        @pl.when(ctx >= gap)
        def _():
            greet(ctx - gap, me)

        @pl.when(ctx < places - gap)
        def _():
            greet(ctx + gap, me)

    own_load.start()
    for load in zx_loads:
        load.start()
    bc_load.start()
    for load in out_loads:
        load.start()

    lane = lax.broadcasted_iota(jnp.int32, (1, QUAD), 1)
    row_id = lax.broadcasted_iota(jnp.int32, (BLOCK, BLOCK), 0)
    col_id = lax.broadcasted_iota(jnp.int32, (BLOCK, BLOCK), 1)

    def widened(per_head):
        high = per_head.astype(BF16).astype(F32)
        stack = jnp.concatenate([high, per_head - high, jnp.zeros((96, BLOCK), F32)], axis=0)
        return stack.T.astype(BF16)

    def split(j):
        flat = wraw.at[j].reshape(2 * width, LANES)

        def step(i, carry):
            for u in range(2):
                at = pl.multiple_of((2 * i + u) * CUT, CUT)
                wf[u] = flat[pl.ds(pl.multiple_of(2 * at, 2 * CUT), 2 * CUT), :].astype(F32)
                for g in range(2):
                    first = g * inner + j * LANES
                    wzx[pl.ds(at, CUT), first : first + LANES] = wf[
                        u, pl.ds(g, CUT, stride=2), :
                    ].astype(BF16)
            return carry

        lax.fori_loop(0, width // (2 * CUT), step, 0)

    dt_wide = jnp.concatenate(
        [wdt_in[...].astype(F32), jnp.zeros((128 - heads, width), F32)], axis=0
    )
    wdt[...] = dt_wide.T.astype(BF16)
    few = lax.broadcasted_iota(jnp.int32, (8, 128), 1)
    bias_row = jnp.zeros((8, 128), F32)
    for h in range(heads):
        bias_row = jnp.where(few == h, dtb[h], bias_row)
    dtrow[...] = bias_row
    wide = lax.broadcasted_iota(jnp.int32, (8, inner), 1)
    skip_row = jnp.zeros((8, inner), F32)
    for h in range(heads):
        skip_row = jnp.where(wide >= h * HEADDIM, skip[h], skip_row)
    skrow[...] = skip_row
    which = lax.broadcasted_iota(jnp.int32, (128, inner), 0)
    which = jnp.where(which >= 16, which - 16, which)
    across = lax.broadcasted_iota(jnp.int32, (128, inner), 1)
    within = (across >= which * HEADDIM) & (across < (which + 1) * HEADDIM)
    expand[...] = jnp.where(within, 1.0, 0.0).astype(BF16)
    st[...] = jnp.zeros_like(st)
    dsum[...] = jnp.zeros_like(dsum)
    ldp[...] = jnp.zeros_like(ldp)
    tri = jnp.where(row_id <= col_id, 1.0, 0.0).astype(F32)

    def decays(c, carry):
        here = pl.ds(pl.multiple_of(c * BLOCK, BLOCK), BLOCK)
        ldp[0:heads, :] = ld_in[:, here]
        drow = jnp.dot(ldp[...], tri, preferred_element_type=F32, precision=lax.Precision.HIGHEST)
        dcol = jnp.concatenate([drow, jnp.zeros((112, BLOCK), F32)], axis=0).T
        drow_all[c] = drow
        dcol_all[here, :] = dcol
        tl[c] = dsum[...]
        for q in range(quads):
            span = slice(q * QUAD, (q + 1) * QUAD)
            total = spread(lambda i: dcol[BLOCK - 1 : BLOCK, i : i + 1], q * PER, lane, 1)
            et[c, :, span] = jnp.broadcast_to(jnp.exp(total), (8, QUAD))
            dsum[:, span] = dsum[:, span] + total
        return carry

    lax.fori_loop(0, chunks, decays, 0)

    below = lax.div(ctx + places - 1, places)
    above = lax.div(2 * places - 2 - ctx, places)
    hops = 0
    for gap in (2, 4):
        hops = hops + lax.div(ctx + places - gap, places)
        hops = hops + lax.div(2 * places - 1 - gap - ctx, places)
    pl.semaphore_wait(barrier, 3 + 4 * (below + above) + hops)

    def src_rows(c):
        return hidden.at[pl.ds(pl.multiple_of(c * BLOCK, BLOCK), BLOCK)]

    def slot(h, c):
        return xg.at[h, pl.ds(pl.multiple_of(HALO + c * BLOCK, HALO), BLOCK)]

    def to_y(c):
        return remote(src_rows(c), slot(me, c), ys.at[c], yr.at[c], ctx, other)

    def to_p(c):
        return remote(src_rows(c), slot(me, c), ps.at[c], pr.at[c], ctx, partner)

    def forward(c):
        return remote(slot(other, c), slot(other, c), fs.at[c], fr.at[c], ctx, partner)

    def forwarded(c):
        return remote(slot(diag, c), slot(diag, c), fs.at[c], fr.at[c], ctx, partner)

    def halo(h, sender):
        return remote(
            hidden.at[pl.ds(rows - HALO, HALO)],
            xg.at[sender, pl.ds(0, HALO)],
            hs.at[h],
            hr.at[sender],
            ctx + 1,
            h,
        )

    decay_copy = remote(dsum, got_d, ds_.at[0], dr_.at[0], mate, me)
    decay_pair_copy = remote(dpair, got_dp, ds_.at[1], dr_.at[1], ctx + 2, me)

    @pl.when(ctx < places - 1)
    def _():
        for h in range(4):
            halo(h, me).start()

    for c in range(chunks):
        to_y(c).start()
    for c in range(chunks):
        to_p(c).start()

    @pl.when(ctx == 0)
    def _():
        xg[:, 0:HALO, :] = jnp.zeros((4, HALO, feat), BF16)

    decay_copy.start()

    for j in range(tiles):
        zx_loads[j].wait()
        split(j)

    bc_load.wait()
    own_load.wait()
    decay_copy.wait_recv()
    dpair[...] = dsum[...] + got_d[...]

    @pl.when(ctx < places - 2)
    def _():
        decay_pair_copy.start()

    @pl.when(ctx > 0)
    def _():
        for h in range(4):
            halo(0, h).wait_recv()

    def normalised(at, count):
        vals = [xg[j, at, :].astype(F32) for j in range(4)]
        total = sum(jnp.sum(v * v, axis=-1, keepdims=True) for v in vals)
        scale = lax.rsqrt(total / width + eps)
        return [
            (vals[j] * scale * gain[j * feat : (j + 1) * feat].reshape(1, feat)).astype(BF16)
            for j in range(4)
        ]

    head_rows = jnp.concatenate(normalised(pl.ds(0, HALO), HALO), axis=1)
    for s in range(quads):
        tail[:, s * QUAD : (s + 1) * QUAD] = dot(
            head_rows, wzx[:, inner + s * QUAD : inner + (s + 1) * QUAD]
        )
    tail[:, inner : inner + 2 * STATE] = dot(head_rows, wbc[...])

    def convolved(raw, span, taps):
        ext = jnp.concatenate([tail[:, span], raw], axis=0)
        summed = taps[CONV : CONV + 1, :] + taps[CONV - 1 : CONV, :] * ext
        for back_by in range(1, CONV):
            at = CONV - 1 - back_by
            summed = summed + taps[at : at + 1, :] * pltpu.roll(ext, back_by, 0)
        tail[:, span] = raw[BLOCK - HALO :, :]
        return silu(summed[HALO:, :])

    def inside(c):
        here = pl.ds(pl.multiple_of(c * BLOCK, BLOCK), BLOCK)
        cc = cm[here, :]
        low = slice(0, HALF)
        high = slice(HALF, BLOCK)
        at = pl.multiple_of(c * BLOCK, BLOCK)
        top = pl.ds(at, HALF)
        bottom = pl.ds(at + HALF, HALF)
        scores = lax.dot_general(
            cc, bm[here, :], (((1,), (1,)), ((), ())), preferred_element_type=F32
        )
        s_top = scores[low, low]
        s_side = scores[high, low]
        s_diag = scores[high, high]
        causal = row_id[low, low] >= col_id[low, low]
        grown = widened(jnp.exp(drow_all[c]))
        for q in range(quads):
            span = slice(q * QUAD, (q + 1) * QUAD)
            xq = xc[here, span]
            tops = []
            bottoms = []
            parts = []
            for k in range(PER):
                h = q * PER + k
                d_top = dcol_all[top, h : h + 1]
                d_bottom = dcol_all[bottom, h : h + 1]
                e_low = e_keep[c, h : h + 1, low]
                e_high = e_keep[c, h : h + 1, high]
                tops.append((s_top * jnp.exp(jnp.where(causal, d_top - e_low, -jnp.inf))).astype(BF16))
                bottoms.append((s_side * jnp.exp(d_bottom - e_low)).astype(BF16))
                bottoms.append(
                    (s_diag * jnp.exp(jnp.where(causal, d_bottom - e_high, -jnp.inf))).astype(BF16)
                )
                mine = (lane >= k * HEADDIM) & (lane < (k + 1) * HEADDIM)
                parts.append(jnp.where(mine, xq, jnp.zeros_like(xq)))
            y_top = dot(
                jnp.concatenate(tops, axis=1),
                jnp.concatenate([part[low, :] for part in parts], axis=0),
            )
            y_bottom = dot(jnp.concatenate(bottoms, axis=1), jnp.concatenate(parts, axis=0))
            y = jnp.concatenate([y_top, y_bottom], axis=0)
            growth = dot(grown, expand[:, span])
            y = y + growth * dot(cc, ent[c, :, span])
            yl[here, span] = y + skrow[0:1, span] * xq.astype(F32)
            gr[here, span] = growth * jnp.exp(tl[c, 0:1, span])

    def gates(c):
        here = pl.ds(pl.multiple_of(c * BLOCK, BLOCK), BLOCK)
        opened = silu(dot(nrm[here, :], wzx[:, 0:inner]))
        for q in range(quads):
            span = slice(q * QUAD, (q + 1) * QUAD)
            g = opened[:, span]
            yl[here, span] = yl[here, span] * g
            gr[here, span] = gr[here, span] * g

    def state_copy(i):
        return remote(snd_s.at[i], got_s.at[i], cs.at[i], cr.at[i], mate, me)

    def advance(c, last):
        to_p(c).wait_recv()
        forwarded(c).wait_recv()
        here = pl.ds(pl.multiple_of(c * BLOCK, BLOCK), BLOCK)
        pieces = normalised(pl.ds(pl.multiple_of(HALO + c * BLOCK, HALO), BLOCK), BLOCK)
        for j in range(4):
            nrm[here, j * feat : (j + 1) * feat] = pieces[j]
        normed = nrm[here, :]
        bc = convolved(dot(normed, wbc[...]), slice(inner, inner + 2 * STATE), taps_bc[...])
        b = bc[:, :STATE].astype(BF16)
        cc = bc[:, STATE:].astype(BF16)
        cm[here, :] = cc
        raw_step = dot(normed, wdt[...]) + dtrow[0:1, :]
        step = jnp.maximum(raw_step, 0.0) + jnp.log1p(jnp.exp(-jnp.abs(raw_step)))
        srow = step.T[0:16, :]
        drow = drow_all[c]
        e_row = drow - jnp.log(srow)
        e_keep[c] = e_row
        wrow = jnp.exp(drow[:, BLOCK - 1 : BLOCK] - e_row)
        bm[here, :] = b
        b_t = b.astype(F32).T.astype(BF16)
        weights = widened(wrow)
        raws = dot(normed, wzx[:, inner : 2 * inner])
        for q in range(quads):
            span = slice(q * QUAD, (q + 1) * QUAD)
            raw = raws[:, span]
            xq = convolved(raw, span, taps_x[:, span]).astype(BF16)
            xc[here, span] = xq
            weighted = (xq.astype(F32) * dot(weights, expand[:, span])).astype(BF16)
            ent[c, :, span] = st[:, span].astype(BF16)
            now = et[c, 0:1, span] * st[:, span] + dot(b_t, weighted)
            st[:, span] = now
            if last:
                snd_s[q] = jnp.where(odd == 0, now[:, GROUP:], now[:, :GROUP]).astype(BF16)
                state_copy(q).start()

    def arrive(c):
        to_y(c).wait_recv()
        forward(c).start()

    def first(c, carry):
        advance(c, False)
        arrive(c + 1)

        @pl.when(pair > 0)
        def _():
            inside(c)

        return carry

    arrive(0)
    lax.fori_loop(0, chunks - 1, first, 0)
    advance(chunks - 1, True)

    turns = inner // GROUP // 2

    def lanes_of(g):
        return pl.ds(pl.multiple_of(g * GROUP, GROUP), GROUP)

    def enter_copy(i):
        return remote(snd_e.at[i], got_e.at[i], es.at[i], er.at[i], ctx + 2, me)

    def leap_copy(i):
        return remote(snd_e.at[i], got_t.at[i], ts.at[i], tr.at[i], ctx + 4, me)

    def back_copy(i):
        return remote(snd_b.at[i], back.at[i], bs.at[i], br.at[i], mate, me)

    def pair_parts(i):
        at = lanes_of(2 * i + odd)
        mine, theirs = st[:, at], got_s[i].astype(F32)
        earlier = jnp.where(odd == 0, mine, theirs)
        later = jnp.where(odd == 0, theirs, mine)
        d_earlier = jnp.where(odd == 0, dsum[0:1, at], got_d[0:1, at])
        d_later = jnp.where(odd == 0, got_d[0:1, at], dsum[0:1, at])
        return at, earlier, later, d_earlier, d_later

    def hand_back(i, at, entered, earlier, d_earlier):
        after = jnp.exp(d_earlier) * entered + earlier
        snd_b[i] = jnp.where(odd == 0, after, entered).astype(BF16)
        inc[:, at] = jnp.where(odd == 0, entered, after).astype(BF16)
        back_copy(i).start()

    def relay_even():
        for i in range(turns):
            state_copy(i).wait_recv()
            at, earlier, later, d_earlier, d_later = pair_parts(i)

            @pl.when(ctx < places - 2)
            def _():
                snd_e[i] = (jnp.exp(d_later) * earlier + later).astype(BF16)
                enter_copy(i).start()

    def finish_even():
        for i in range(turns):

            @pl.when(pair > 0)
            def _():
                enter_copy(i).wait_recv()

            at, earlier, later, d_earlier, d_later = pair_parts(i)
            hand_back(i, at, got_e[i].astype(F32), earlier, d_earlier)

    def relay_odd():
        for i in range(turns):
            state_copy(i).wait_recv()
            enter_copy(i).wait_recv()
            at, earlier, later, d_earlier, d_later = pair_parts(i)

            @pl.when(pair > 1)
            def _():
                leap_copy(i).wait_recv()

            entered = jnp.exp(got_dp[0:1, at]) * got_t[i].astype(F32) + got_e[i].astype(F32)

            @pl.when(ctx < places - 2)
            def _():
                whole = jnp.exp(d_earlier + d_later) * entered + jnp.exp(d_later) * earlier + later
                snd_e[i] = whole.astype(BF16)

                @pl.when(ctx < places - 4)
                def _():
                    leap_copy(i).start()

                enter_copy(i).start()

            hand_back(i, at, entered, earlier, d_earlier)

    @pl.when(ctx >= 2)
    def _():
        decay_pair_copy.wait_recv()

    @pl.when(ctx < 2)
    def _():
        got_e[...] = jnp.zeros_like(got_e)
        got_dp[...] = jnp.zeros_like(got_dp)

    @pl.when(pair <= 1)
    def _():
        got_t[...] = jnp.zeros_like(got_t)

    inside(chunks - 1)

    @pl.when(odd_pair == 0)
    def _():
        relay_even()

    @pl.when(pair == 0)
    def _():
        finish_even()

    @pl.when(pair == 1)
    def _():
        relay_odd()

    half = chunks // 2

    def gate_step(c, carry):
        gates(c)
        return carry

    @pl.when(pair > 0)
    def _():
        lax.fori_loop(0, half, gate_step, 0)

    @pl.when(pair > 0)
    def _():
        lax.fori_loop(half, chunks, gate_step, 0)

    @pl.when((odd_pair == 1) & (pair > 1))
    def _():
        relay_odd()

    @pl.when((odd_pair == 0) & (pair > 0))
    def _():
        finish_even()

    for load in out_loads:
        load.wait()

    for i in range(turns):
        back_copy(i).wait_recv()
        inc[:, lanes_of(2 * i + 1 - odd)] = back[i]

    def piece_copy(k, s):
        return remote(send_p.at[k, s], recv_p.at[k, s], rs.at[k, s], rr.at[k, s], ctx, partner)

    def far_copy(s):
        return remote(send_y.at[s], recv_y.at[s], zs.at[s], zr.at[s], ctx, other)

    def square_near(s):
        return remote(sq_own.at[s, pl.ds(0, 1)], sq_p.at[s, pl.ds(0, 1)], qs.at[0, s], qr.at[0, s], ctx, partner)

    def square_far(s):
        return remote(sq_sum.at[s, pl.ds(0, 1)], sq_far.at[s, pl.ds(0, 1)], qs.at[1, s], qr.at[1, s], ctx, other)

    def combine(s):
        piece_copy(0, s).wait_recv()
        send_y[s] = (held[s] + recv_p[0, s].astype(F32)).astype(BF16)
        far_copy(s).start()
        square_near(s).wait_recv()
        sq_sum[s, 0:1, :] = sq_own[s, 0:1, :] + sq_p[s, 0:1, :]
        square_far(s).start()

    def second(s, carry):
        @pl.when((pair == 0) & (lax.rem(s, BLOCK // SUB) == 0))
        def _():
            c = lax.div(s, BLOCK // SUB)

            @pl.when(c < chunks - 1)
            def _():
                inside(c)

            gates(c)

        here = pl.ds(pl.multiple_of(s * SUB, SUB), SUB)
        squares = jnp.zeros((SUB, 1), F32)
        cc = cm[here, :]
        for q in range(quads):
            span = slice(q * QUAD, (q + 1) * QUAD)
            gated = yl[here, span] + gr[here, span] * dot(cc, inc[:, span])
            squares = squares + jnp.sum(gated * gated, axis=-1, keepdims=True)
            gb[:, span] = (gated * out_gain[span].reshape(1, QUAD)).astype(BF16)
        g = gb[...]
        across = dot(g, wout[:, 0 : 2 * feat])
        send_p[0, s] = across[:, 0:feat].astype(BF16)
        piece_copy(0, s).start()
        sq_own[s, 0:1, :] = jnp.broadcast_to(squares, (SUB, 128)).T[0:1, :]
        square_near(s).start()
        staying = dot(g, wout[:, 2 * feat : 4 * feat])
        send_p[1, s] = staying[:, 0:feat].astype(BF16)
        piece_copy(1, s).start()
        own[s] = staying[:, feat : 2 * feat]
        held[s] = across[:, feat : 2 * feat]

        @pl.when(s == 0)
        def _():
            combine(s)

        @pl.when(s > 1)
        def _():
            combine(s - 1)

        return carry

    lax.fori_loop(0, subs, second, 0)
    combine(subs - 1)

    def leave(s):
        here = pl.ds(pl.multiple_of(s * SUB, SUB), SUB)
        return pltpu.make_async_copy(ready.at[here], out.at[here], out_sem.at[s])

    def third(s, carry):
        here = pl.ds(pl.multiple_of(s * SUB, SUB), SUB)
        piece_copy(1, s).wait_recv()
        mine = own[s] + recv_p[1, s].astype(F32)
        square_far(s).wait_recv()
        scale_row = lax.rsqrt((sq_sum[s, 0:1, :] + sq_far[s, 0:1, :]) / (4 * inner) + eps)
        scale = jnp.broadcast_to(scale_row, (128, SUB)).T[:, 0:1]
        far_copy(s).wait_recv()
        ready[here, :] = ((mine + recv_y[s].astype(F32)) * scale).astype(BF16)
        leave(s).start()
        return carry

    lax.fori_loop(0, subs, third, 0)

    for c in range(chunks):
        to_y(c).wait_send()
        to_p(c).wait_send()
        forward(c).wait_send()

    decay_copy.wait_send()
    for i in range(turns):
        state_copy(i).wait_send()
        back_copy(i).wait_send()

    @pl.when(ctx < places - 2)
    def _():
        decay_pair_copy.wait_send()
        for i in range(turns):
            enter_copy(i).wait_send()

    @pl.when((odd_pair == 1) & (ctx < places - 4))
    def _():
        for i in range(turns):
            leap_copy(i).wait_send()

    def drain(s, carry):
        piece_copy(0, s).wait_send()
        piece_copy(1, s).wait_send()
        leave(s).wait()
        square_near(s).wait_send()
        far_copy(s).wait_send()
        square_far(s).wait_send()
        return carry

    lax.fori_loop(0, subs, drain, 0)

    @pl.when(ctx < places - 1)
    def _():
        for h in range(4):
            halo(h, me).wait_send()


def per_device(
    places,
    hidden,
    norm_gain,
    zx_weight,
    bc_weight,
    dt_weight,
    conv_x,
    conv_bc,
    dt_bias,
    log_decay,
    skip_gain,
    out_gain,
    out_weight,
):
    rows, feat = hidden.shape
    width = zx_weight.shape[0]
    inner = zx_weight.shape[2]
    turns = inner // GROUP // 2
    tiles = inner // LANES
    chunks = rows // BLOCK
    subs = rows // SUB
    any_spec = pl.BlockSpec(memory_space=pl.ANY)
    vmem = pl.BlockSpec(memory_space=pltpu.VMEM)
    smem = pl.BlockSpec(memory_space=pltpu.SMEM)
    dma = pltpu.SemaphoreType.DMA
    return pl.pallas_call(
        functools.partial(kernel, places),
        out_shape=jax.ShapeDtypeStruct((rows, feat), BF16),
        in_specs=[any_spec] * 4 + [vmem] * 4 + [smem, vmem, smem, vmem],
        out_specs=any_spec,
        scratch_shapes=[
            pltpu.VMEM((4, HALO + rows, feat), BF16),
            pltpu.VMEM((tiles, width, 2, LANES), BF16),
            pltpu.VMEM((2, 2 * CUT, LANES), F32),
            pltpu.VMEM((width, 2 * inner), BF16),
            pltpu.VMEM((width, 2 * STATE), BF16),
            pltpu.VMEM((inner, width), BF16),
            pltpu.VMEM((width, 128), BF16),
            pltpu.VMEM((8, 128), F32),
            pltpu.VMEM((8, inner), F32),
            pltpu.VMEM((rows, width), BF16),
            pltpu.VMEM((HALO, inner + 2 * STATE), F32),
            pltpu.VMEM((16, BLOCK), F32),
            pltpu.VMEM((rows, inner), BF16),
            pltpu.VMEM((rows, STATE), BF16),
            pltpu.VMEM((rows, inner), F32),
            pltpu.VMEM((rows, inner), F32),
            pltpu.VMEM((chunks, STATE, inner), BF16),
            pltpu.VMEM((chunks, 8, inner), F32),
            pltpu.VMEM((chunks, 8, inner), F32),
            pltpu.VMEM((rows, 128), F32),
            pltpu.VMEM((128, inner), BF16),
            pltpu.VMEM((chunks, 16, BLOCK), F32),
            pltpu.VMEM((STATE, inner), F32),
            pltpu.VMEM((8, inner), F32),
            pltpu.VMEM((rows, STATE), BF16),
            pltpu.VMEM((chunks, 16, BLOCK), F32),
            pltpu.VMEM((8, inner), F32),
            pltpu.VMEM((8, inner), F32),
            pltpu.VMEM((8, inner), F32),
            pltpu.VMEM((turns, STATE, GROUP), BF16),
            pltpu.VMEM((turns, STATE, GROUP), BF16),
            pltpu.VMEM((turns, STATE, GROUP), BF16),
            pltpu.VMEM((turns, STATE, GROUP), BF16),
            pltpu.VMEM((turns, STATE, GROUP), BF16),
            pltpu.VMEM((turns, STATE, GROUP), BF16),
            pltpu.VMEM((turns, STATE, GROUP), BF16),
            pltpu.VMEM((STATE, inner), BF16),
            pltpu.VMEM((SUB, inner), BF16),
            pltpu.VMEM((2, subs, SUB, feat), BF16),
            pltpu.VMEM((2, subs, SUB, feat), BF16),
            pltpu.VMEM((subs, SUB, feat), F32),
            pltpu.VMEM((subs, SUB, feat), F32),
            pltpu.VMEM((rows, feat), BF16),
            pltpu.VMEM((subs, SUB, feat), BF16),
            pltpu.VMEM((subs, SUB, feat), BF16),
            pltpu.VMEM((subs, 8, SUB), F32),
            pltpu.VMEM((subs, 8, SUB), F32),
            pltpu.VMEM((subs, 8, SUB), F32),
            pltpu.VMEM((subs, 8, SUB), F32),
            dma((6 + tiles,)),
            dma((chunks,)),
            dma((chunks,)),
            dma((chunks,)),
            dma((chunks,)),
            dma((chunks,)),
            dma((chunks,)),
            dma((4,)),
            dma((4,)),
            dma((2,)),
            dma((2,)),
            dma((turns,)),
            dma((turns,)),
            dma((turns,)),
            dma((turns,)),
            dma((turns,)),
            dma((turns,)),
            dma((turns,)),
            dma((turns,)),
            dma((2, subs)),
            dma((2, subs)),
            dma((subs,)),
            dma((subs,)),
            dma((2, subs)),
            dma((2, subs)),
            dma((subs,)),
        ],
        compiler_params=pltpu.CompilerParams(
            collective_id=0, has_side_effects=True, vmem_limit_bytes=63000000
        ),
        name="mixer",
    )(
        hidden,
        zx_weight,
        bc_weight,
        out_weight,
        norm_gain,
        dt_weight.T,
        conv_x,
        conv_bc,
        dt_bias,
        log_decay.T,
        skip_gain,
        out_gain,
    )


def solution(mesh):
    placed = (
        P("ctx", "head"),
        P(),
        P(None, None, "head"),
        P(),
        P(None, "head"),
        P(None, "head"),
        P(),
        P("head"),
        P("ctx", "head"),
        P("head"),
        P("head"),
        P("head", None),
    )
    return jax.shard_map(
        functools.partial(per_device, mesh.shape["ctx"]),
        mesh=mesh,
        in_specs=placed,
        out_specs=P("ctx", "head"),
        check_vma=False,
    )
```

```python
import functools

import jax
import jax.numpy as jnp
from jax import lax
from jax.experimental import pallas as pl
from jax.experimental.pallas import tpu as pltpu
from jax.sharding import PartitionSpec as P

HEADDIM = 64
STATE = 128
CONV = 4
BLOCK = 256
HALO = 16
QUAD = 256
GROUP = 128
CUTS = 2
PIECE = STATE // CUTS
PER = QUAD // HEADDIM
SUB = 128
HALF = BLOCK // 2
LANES = 128
CUT = 256

eps = 1e-05
F32 = jnp.float32
BF16 = jnp.bfloat16


def dot(a, b):
    return jnp.dot(a, b, preferred_element_type=F32)


def silu(v):
    half = 0.5 * v
    return half + half * jnp.tanh(half)


def spread(column_of, first, lane, rows):
    out = None
    for k in range(PER):
        piece = jnp.broadcast_to(column_of(first + k), (rows, QUAD))
        out = piece if out is None else jnp.where(lane >= k * HEADDIM, piece, out)
    return out


def kernel(
    places,
    hidden,
    wzx_hbm,
    wbc_hbm,
    wout_hbm,
    gain,
    wdt_in,
    taps_x,
    taps_bc,
    dtb,
    ld_in,
    skip,
    out_gain,
    out,
    xg,
    wraw,
    wf,
    wzx,
    wbc,
    wout,
    wdt,
    dtrow,
    skrow,
    nrm,
    tail,
    ldp,
    xc,
    cm,
    yl,
    gr,
    ent,
    tl,
    et,
    dcol_all,
    expand,
    drow_all,
    st,
    dsum,
    bm,
    e_keep,
    got_d,
    dpair,
    got_dp,
    got_s,
    snd_s,
    got_e,
    got_t,
    snd_e,
    snd_b,
    back,
    inc,
    gb,
    send_p,
    recv_p,
    own,
    held,
    ready,
    send_y,
    recv_y,
    sq_own,
    sq_p,
    sq_sum,
    sq_far,
    load_sem,
    ys,
    yr,
    ps,
    pr,
    fs,
    fr,
    hs,
    hr,
    ds_,
    dr_,
    cs,
    cr,
    es,
    er,
    ts,
    tr,
    bs,
    br,
    rs,
    rr,
    zs,
    zr,
    qs,
    qr,
    out_sem,
):
    rows, feat = hidden.shape
    width = 4 * feat
    inner = wzx.shape[1] // 2
    heads = inner // HEADDIM
    quads = inner // QUAD
    chunks = rows // BLOCK
    subs = rows // SUB
    tiles = inner // LANES
    ctx = lax.axis_index("ctx")
    me = lax.axis_index("head")
    partner = me + 1 - 2 * lax.rem(me, 2)
    other = lax.rem(me + 2, 4)
    diag = lax.rem(partner + 2, 4)
    odd = lax.rem(ctx, 2)
    mate = ctx + 1 - 2 * odd
    pair = lax.div(ctx, 2)
    odd_pair = lax.rem(pair, 2)
    MESH = pl.DeviceIdType.MESH

    def remote(src, dst, ss, rsem, c, h):
        return pltpu.make_async_remote_copy(
            src_ref=src, dst_ref=dst, send_sem=ss, recv_sem=rsem, device_id=(c, h), device_id_type=MESH
        )

    def columns(h):
        return pl.ds(pl.multiple_of(h * feat, 128), feat)

    own_load = pltpu.make_async_copy(hidden, xg.at[me, pl.ds(HALO, rows)], load_sem.at[0])
    bc_load = pltpu.make_async_copy(wbc_hbm, wbc, load_sem.at[1])
    zx_loads = [
        pltpu.make_async_copy(
            wzx_hbm.at[:, :, pl.ds(j * LANES, LANES)], wraw.at[j], load_sem.at[6 + j]
        )
        for j in range(tiles)
    ]
    out_loads = [
        pltpu.make_async_copy(
            wout_hbm.at[:, columns(h)], wout.at[:, pl.ds(k * feat, feat)], load_sem.at[2 + k]
        )
        for k, h in enumerate((diag, other, partner, me))
    ]

    barrier = pltpu.get_barrier_semaphore()

    def greet(c, h):
        pl.semaphore_signal(barrier, inc=1, device_id=(c, h), device_id_type=MESH)

    for h in (partner, other, diag):
        greet(ctx, h)

    @pl.when(ctx > 0)
    def _():
        for h in range(4):
            greet(ctx - 1, h)

    @pl.when(ctx < places - 1)
    def _():
        for h in range(4):
            greet(ctx + 1, h)

    for gap in (2, 4):

        @pl.when(ctx >= gap)
        def _():
            greet(ctx - gap, me)

        @pl.when(ctx < places - gap)
        def _():
            greet(ctx + gap, me)

    own_load.start()
    for load in zx_loads:
        load.start()
    bc_load.start()
    for load in out_loads:
        load.start()

    lane = lax.broadcasted_iota(jnp.int32, (1, QUAD), 1)
    row_id = lax.broadcasted_iota(jnp.int32, (BLOCK, BLOCK), 0)
    col_id = lax.broadcasted_iota(jnp.int32, (BLOCK, BLOCK), 1)

    def widened(per_head):
        high = per_head.astype(BF16).astype(F32)
        stack = jnp.concatenate([high, per_head - high, jnp.zeros((96, BLOCK), F32)], axis=0)
        return stack.T.astype(BF16)

    def split(j):
        flat = wraw.at[j].reshape(2 * width, LANES)

        def step(i, carry):
            for u in range(2):
                at = pl.multiple_of((2 * i + u) * CUT, CUT)
                wf[u] = flat[pl.ds(pl.multiple_of(2 * at, 2 * CUT), 2 * CUT), :].astype(F32)
                for g in range(2):
                    first = g * inner + j * LANES
                    wzx[pl.ds(at, CUT), first : first + LANES] = wf[
                        u, pl.ds(g, CUT, stride=2), :
                    ].astype(BF16)
            return carry

        lax.fori_loop(0, width // (2 * CUT), step, 0)

    dt_wide = jnp.concatenate(
        [wdt_in[...].astype(F32), jnp.zeros((128 - heads, width), F32)], axis=0
    )
    wdt[...] = dt_wide.T.astype(BF16)
    few = lax.broadcasted_iota(jnp.int32, (8, 128), 1)
    bias_row = jnp.zeros((8, 128), F32)
    for h in range(heads):
        bias_row = jnp.where(few == h, dtb[h], bias_row)
    dtrow[...] = bias_row
    wide = lax.broadcasted_iota(jnp.int32, (8, inner), 1)
    skip_row = jnp.zeros((8, inner), F32)
    for h in range(heads):
        skip_row = jnp.where(wide >= h * HEADDIM, skip[h], skip_row)
    skrow[...] = skip_row
    which = lax.broadcasted_iota(jnp.int32, (128, inner), 0)
    which = jnp.where(which >= 16, which - 16, which)
    across = lax.broadcasted_iota(jnp.int32, (128, inner), 1)
    within = (across >= which * HEADDIM) & (across < (which + 1) * HEADDIM)
    expand[...] = jnp.where(within, 1.0, 0.0).astype(BF16)
    st[...] = jnp.zeros_like(st)
    dsum[...] = jnp.zeros_like(dsum)
    ldp[...] = jnp.zeros_like(ldp)
    tri = jnp.where(row_id <= col_id, 1.0, 0.0).astype(F32)

    def decays(c, carry):
        here = pl.ds(pl.multiple_of(c * BLOCK, BLOCK), BLOCK)
        ldp[0:heads, :] = ld_in[:, here]
        drow = jnp.dot(ldp[...], tri, preferred_element_type=F32, precision=lax.Precision.HIGHEST)
        dcol = jnp.concatenate([drow, jnp.zeros((112, BLOCK), F32)], axis=0).T
        drow_all[c] = drow
        dcol_all[here, :] = dcol
        tl[c] = dsum[...]
        for q in range(quads):
            span = slice(q * QUAD, (q + 1) * QUAD)
            total = spread(lambda i: dcol[BLOCK - 1 : BLOCK, i : i + 1], q * PER, lane, 1)
            et[c, :, span] = jnp.broadcast_to(jnp.exp(total), (8, QUAD))
            dsum[:, span] = dsum[:, span] + total
        return carry

    lax.fori_loop(0, chunks, decays, 0)

    below = lax.div(ctx + places - 1, places)
    above = lax.div(2 * places - 2 - ctx, places)
    hops = 0
    for gap in (2, 4):
        hops = hops + lax.div(ctx + places - gap, places)
        hops = hops + lax.div(2 * places - 1 - gap - ctx, places)
    pl.semaphore_wait(barrier, 3 + 4 * (below + above) + hops)

    def src_rows(c):
        return hidden.at[pl.ds(pl.multiple_of(c * BLOCK, BLOCK), BLOCK)]

    def slot(h, c):
        return xg.at[h, pl.ds(pl.multiple_of(HALO + c * BLOCK, HALO), BLOCK)]

    def to_y(c):
        return remote(src_rows(c), slot(me, c), ys.at[c], yr.at[c], ctx, other)

    def to_p(c):
        return remote(src_rows(c), slot(me, c), ps.at[c], pr.at[c], ctx, partner)

    def forward(c):
        return remote(slot(other, c), slot(other, c), fs.at[c], fr.at[c], ctx, partner)

    def forwarded(c):
        return remote(slot(diag, c), slot(diag, c), fs.at[c], fr.at[c], ctx, partner)

    def halo(h, sender):
        return remote(
            hidden.at[pl.ds(rows - HALO, HALO)],
            xg.at[sender, pl.ds(0, HALO)],
            hs.at[h],
            hr.at[sender],
            ctx + 1,
            h,
        )

    decay_copy = remote(dsum, got_d, ds_.at[0], dr_.at[0], mate, me)
    decay_pair_copy = remote(dpair, got_dp, ds_.at[1], dr_.at[1], ctx + 2, me)

    @pl.when(ctx < places - 1)
    def _():
        for h in range(4):
            halo(h, me).start()

    for c in range(chunks):
        to_y(c).start()
    for c in range(chunks):
        to_p(c).start()

    @pl.when(ctx == 0)
    def _():
        xg[:, 0:HALO, :] = jnp.zeros((4, HALO, feat), BF16)

    decay_copy.start()

    for j in range(tiles):
        zx_loads[j].wait()
        split(j)

    bc_load.wait()
    own_load.wait()
    decay_copy.wait_recv()
    dpair[...] = dsum[...] + got_d[...]

    @pl.when(ctx < places - 2)
    def _():
        decay_pair_copy.start()

    @pl.when(ctx > 0)
    def _():
        for h in range(4):
            halo(0, h).wait_recv()

    def normalised(at, count):
        vals = [xg[j, at, :].astype(F32) for j in range(4)]
        total = sum(jnp.sum(v * v, axis=-1, keepdims=True) for v in vals)
        scale = lax.rsqrt(total / width + eps)
        return [
            (vals[j] * scale * gain[j * feat : (j + 1) * feat].reshape(1, feat)).astype(BF16)
            for j in range(4)
        ]

    head_rows = jnp.concatenate(normalised(pl.ds(0, HALO), HALO), axis=1)
    for s in range(quads):
        tail[:, s * QUAD : (s + 1) * QUAD] = dot(
            head_rows, wzx[:, inner + s * QUAD : inner + (s + 1) * QUAD]
        )
    tail[:, inner : inner + 2 * STATE] = dot(head_rows, wbc[...])

    def convolved(raw, span, taps):
        ext = jnp.concatenate([tail[:, span], raw], axis=0)
        summed = taps[CONV : CONV + 1, :] + taps[CONV - 1 : CONV, :] * ext
        for back_by in range(1, CONV):
            at = CONV - 1 - back_by
            summed = summed + taps[at : at + 1, :] * pltpu.roll(ext, back_by, 0)
        tail[:, span] = raw[BLOCK - HALO :, :]
        return silu(summed[HALO:, :])

    def inside(c):
        here = pl.ds(pl.multiple_of(c * BLOCK, BLOCK), BLOCK)
        cc = cm[here, :]
        low = slice(0, HALF)
        high = slice(HALF, BLOCK)
        at = pl.multiple_of(c * BLOCK, BLOCK)
        top = pl.ds(at, HALF)
        bottom = pl.ds(at + HALF, HALF)
        scores = lax.dot_general(
            cc, bm[here, :], (((1,), (1,)), ((), ())), preferred_element_type=F32
        )
        s_top = scores[low, low]
        s_side = scores[high, low]
        s_diag = scores[high, high]
        causal = row_id[low, low] >= col_id[low, low]
        growths = dot(widened(jnp.exp(drow_all[c])), expand[...])
        locals_in = dot(cc, ent[c])
        for q in range(quads):
            span = slice(q * QUAD, (q + 1) * QUAD)
            xq = xc[here, span]
            tops = []
            bottoms = []
            parts = []
            for k in range(PER):
                h = q * PER + k
                d_top = dcol_all[top, h : h + 1]
                d_bottom = dcol_all[bottom, h : h + 1]
                e_low = e_keep[c, h : h + 1, low]
                e_high = e_keep[c, h : h + 1, high]
                tops.append((s_top * jnp.exp(jnp.where(causal, d_top - e_low, -jnp.inf))).astype(BF16))
                bottoms.append((s_side * jnp.exp(d_bottom - e_low)).astype(BF16))
                bottoms.append(
                    (s_diag * jnp.exp(jnp.where(causal, d_bottom - e_high, -jnp.inf))).astype(BF16)
                )
                mine = (lane >= k * HEADDIM) & (lane < (k + 1) * HEADDIM)
                parts.append(jnp.where(mine, xq, jnp.zeros_like(xq)))
            y_top = dot(
                jnp.concatenate(tops, axis=1),
                jnp.concatenate([part[low, :] for part in parts], axis=0),
            )
            y_bottom = dot(jnp.concatenate(bottoms, axis=1), jnp.concatenate(parts, axis=0))
            y = jnp.concatenate([y_top, y_bottom], axis=0)
            growth = growths[:, span]
            y = y + growth * locals_in[:, span]
            yl[here, span] = y + skrow[0:1, span] * xq.astype(F32)
            gr[here, span] = growth * jnp.exp(tl[c, 0:1, span])

    def gates(c):
        here = pl.ds(pl.multiple_of(c * BLOCK, BLOCK), BLOCK)
        opened = silu(dot(nrm[here, :], wzx[:, 0:inner]))
        for q in range(quads):
            span = slice(q * QUAD, (q + 1) * QUAD)
            g = opened[:, span]
            yl[here, span] = yl[here, span] * g
            gr[here, span] = gr[here, span] * g

    def state_copy(i):
        return remote(snd_s.at[i], got_s.at[i], cs.at[i], cr.at[i], mate, me)

    def advance(c, last):
        to_p(c).wait_recv()
        forwarded(c).wait_recv()
        here = pl.ds(pl.multiple_of(c * BLOCK, BLOCK), BLOCK)
        pieces = normalised(pl.ds(pl.multiple_of(HALO + c * BLOCK, HALO), BLOCK), BLOCK)
        for j in range(4):
            nrm[here, j * feat : (j + 1) * feat] = pieces[j]
        normed = nrm[here, :]
        bc = convolved(dot(normed, wbc[...]), slice(inner, inner + 2 * STATE), taps_bc[...])
        b = bc[:, :STATE].astype(BF16)
        cc = bc[:, STATE:].astype(BF16)
        cm[here, :] = cc
        raw_step = dot(normed, wdt[...]) + dtrow[0:1, :]
        step = jnp.maximum(raw_step, 0.0) + jnp.log1p(jnp.exp(-jnp.abs(raw_step)))
        srow = step.T[0:16, :]
        drow = drow_all[c]
        e_row = drow - jnp.log(srow)
        e_keep[c] = e_row
        wrow = jnp.exp(drow[:, BLOCK - 1 : BLOCK] - e_row)
        bm[here, :] = b
        b_t = b.astype(F32).T.astype(BF16)
        weights = widened(wrow)
        raws = dot(normed, wzx[:, inner : 2 * inner])
        for q in range(quads):
            span = slice(q * QUAD, (q + 1) * QUAD)
            raw = raws[:, span]
            xq = convolved(raw, span, taps_x[:, span]).astype(BF16)
            xc[here, span] = xq
            weighted = (xq.astype(F32) * dot(weights, expand[:, span])).astype(BF16)
            ent[c, :, span] = st[:, span].astype(BF16)
            now = et[c, 0:1, span] * st[:, span] + dot(b_t, weighted)
            st[:, span] = now
            if last:
                leaving = jnp.where(odd == 0, now[:, GROUP:], now[:, :GROUP]).astype(BF16)
                for r in range(CUTS):
                    snd_s[CUTS * q + r] = leaving[r * PIECE : (r + 1) * PIECE, :]
                    state_copy(CUTS * q + r).start()

    def arrive(c):
        to_y(c).wait_recv()
        forward(c).start()

    def first(c, carry):
        advance(c, False)
        arrive(c + 1)

        @pl.when(pair > 0)
        def _():
            inside(c)

        return carry

    arrive(0)
    lax.fori_loop(0, chunks - 1, first, 0)
    advance(chunks - 1, True)

    turns = CUTS * inner // GROUP // 2

    def rows_of(i):
        return slice(i % CUTS * PIECE, (i % CUTS + 1) * PIECE)

    def lanes_of(g):
        return pl.ds(pl.multiple_of(g * GROUP, GROUP), GROUP)

    def enter_copy(i):
        return remote(snd_e.at[i], got_e.at[i], es.at[i], er.at[i], ctx + 2, me)

    def leap_copy(i):
        return remote(snd_e.at[i], got_t.at[i], ts.at[i], tr.at[i], ctx + 4, me)

    def back_copy(i):
        return remote(snd_b.at[i], back.at[i], bs.at[i], br.at[i], mate, me)

    def pair_parts(i):
        at = lanes_of(2 * (i // CUTS) + odd)
        mine, theirs = st[rows_of(i), at], got_s[i].astype(F32)
        earlier = jnp.where(odd == 0, mine, theirs)
        later = jnp.where(odd == 0, theirs, mine)
        d_earlier = jnp.where(odd == 0, dsum[0:1, at], got_d[0:1, at])
        d_later = jnp.where(odd == 0, got_d[0:1, at], dsum[0:1, at])
        return at, earlier, later, d_earlier, d_later

    def hand_back(i, at, entered, earlier, d_earlier):
        after = jnp.exp(d_earlier) * entered + earlier
        snd_b[i] = jnp.where(odd == 0, after, entered).astype(BF16)
        inc[rows_of(i), at] = jnp.where(odd == 0, entered, after).astype(BF16)
        back_copy(i).start()

    def relay_even():
        for i in range(turns):
            state_copy(i).wait_recv()
            at, earlier, later, d_earlier, d_later = pair_parts(i)

            @pl.when(ctx < places - 2)
            def _():
                snd_e[i] = (jnp.exp(d_later) * earlier + later).astype(BF16)
                enter_copy(i).start()

    def finish_even():
        for i in range(turns):

            @pl.when(pair > 0)
            def _():
                enter_copy(i).wait_recv()

            at, earlier, later, d_earlier, d_later = pair_parts(i)
            hand_back(i, at, got_e[i].astype(F32), earlier, d_earlier)

    def relay_odd():
        for i in range(turns):
            state_copy(i).wait_recv()
            enter_copy(i).wait_recv()
            at, earlier, later, d_earlier, d_later = pair_parts(i)

            @pl.when(pair > 1)
            def _():
                leap_copy(i).wait_recv()

            entered = jnp.exp(got_dp[0:1, at]) * got_t[i].astype(F32) + got_e[i].astype(F32)

            @pl.when(ctx < places - 2)
            def _():
                whole = jnp.exp(d_earlier + d_later) * entered + jnp.exp(d_later) * earlier + later
                snd_e[i] = whole.astype(BF16)

                @pl.when(ctx < places - 4)
                def _():
                    leap_copy(i).start()

                enter_copy(i).start()

            hand_back(i, at, entered, earlier, d_earlier)

    @pl.when(ctx >= 2)
    def _():
        decay_pair_copy.wait_recv()

    @pl.when(ctx < 2)
    def _():
        got_e[...] = jnp.zeros_like(got_e)
        got_dp[...] = jnp.zeros_like(got_dp)

    @pl.when(pair <= 1)
    def _():
        got_t[...] = jnp.zeros_like(got_t)

    @pl.when(pair > 0)
    def _():
        inside(chunks - 1)

    @pl.when(odd_pair == 0)
    def _():
        relay_even()

    @pl.when(pair == 0)
    def _():
        finish_even()

    @pl.when(pair == 1)
    def _():
        relay_odd()

    half = chunks // 2

    def gate_step(c, carry):
        gates(c)
        return carry

    @pl.when(pair > 0)
    def _():
        lax.fori_loop(0, half, gate_step, 0)

    @pl.when(pair > 0)
    def _():
        lax.fori_loop(half, chunks, gate_step, 0)

    @pl.when((odd_pair == 1) & (pair > 1))
    def _():
        relay_odd()

    @pl.when((odd_pair == 0) & (pair > 0))
    def _():
        finish_even()

    for load in out_loads:
        load.wait()

    for i in range(turns):
        back_copy(i).wait_recv()
        inc[rows_of(i), lanes_of(2 * (i // CUTS) + 1 - odd)] = back[i]

    def piece_copy(k, s):
        return remote(send_p.at[k, s], recv_p.at[k, s], rs.at[k, s], rr.at[k, s], ctx, partner)

    def far_copy(s):
        return remote(send_y.at[s], recv_y.at[s], zs.at[s], zr.at[s], ctx, other)

    def square_near(s):
        return remote(sq_own.at[s, pl.ds(0, 1)], sq_p.at[s, pl.ds(0, 1)], qs.at[0, s], qr.at[0, s], ctx, partner)

    def square_far(s):
        return remote(sq_sum.at[s, pl.ds(0, 1)], sq_far.at[s, pl.ds(0, 1)], qs.at[1, s], qr.at[1, s], ctx, other)

    def combine(s):
        piece_copy(0, s).wait_recv()
        send_y[s] = (held[s] + recv_p[0, s].astype(F32)).astype(BF16)
        far_copy(s).start()
        square_near(s).wait_recv()
        sq_sum[s, 0:1, :] = sq_own[s, 0:1, :] + sq_p[s, 0:1, :]
        square_far(s).start()

    def second(s, carry):
        @pl.when((pair == 0) & (lax.rem(s, BLOCK // SUB) == 0))
        def _():
            c = lax.div(s, BLOCK // SUB)

            inside(c)
            gates(c)

        here = pl.ds(pl.multiple_of(s * SUB, SUB), SUB)
        squares = jnp.zeros((SUB, 1), F32)
        entering = dot(cm[here, :], inc[...])
        for q in range(quads):
            span = slice(q * QUAD, (q + 1) * QUAD)
            gated = yl[here, span] + gr[here, span] * entering[:, span]
            squares = squares + jnp.sum(gated * gated, axis=-1, keepdims=True)
            gb[:, span] = (gated * out_gain[span].reshape(1, QUAD)).astype(BF16)
        g = gb[...]
        across = dot(g, wout[:, 0 : 2 * feat])
        send_p[0, s] = across[:, 0:feat].astype(BF16)
        piece_copy(0, s).start()
        sq_own[s, 0:1, :] = jnp.broadcast_to(squares, (SUB, 128)).T[0:1, :]
        square_near(s).start()
        staying = dot(g, wout[:, 2 * feat : 4 * feat])
        send_p[1, s] = staying[:, 0:feat].astype(BF16)
        piece_copy(1, s).start()
        own[s] = staying[:, feat : 2 * feat]
        held[s] = across[:, feat : 2 * feat]

        @pl.when(s == 0)
        def _():
            combine(s)

        @pl.when(s > 1)
        def _():
            combine(s - 1)

        return carry

    lax.fori_loop(0, subs, second, 0)
    combine(subs - 1)

    def leave(s):
        here = pl.ds(pl.multiple_of(s * SUB, SUB), SUB)
        return pltpu.make_async_copy(ready.at[here], out.at[here], out_sem.at[s])

    def third(s, carry):
        here = pl.ds(pl.multiple_of(s * SUB, SUB), SUB)
        piece_copy(1, s).wait_recv()
        mine = own[s] + recv_p[1, s].astype(F32)
        square_far(s).wait_recv()
        scale_row = lax.rsqrt((sq_sum[s, 0:1, :] + sq_far[s, 0:1, :]) / (4 * inner) + eps)
        scale = jnp.broadcast_to(scale_row, (128, SUB)).T[:, 0:1]
        far_copy(s).wait_recv()
        ready[here, :] = ((mine + recv_y[s].astype(F32)) * scale).astype(BF16)
        leave(s).start()
        return carry

    lax.fori_loop(0, subs, third, 0)

    for c in range(chunks):
        to_y(c).wait_send()
        to_p(c).wait_send()
        forward(c).wait_send()

    decay_copy.wait_send()
    for i in range(turns):
        state_copy(i).wait_send()
        back_copy(i).wait_send()

    @pl.when(ctx < places - 2)
    def _():
        decay_pair_copy.wait_send()
        for i in range(turns):
            enter_copy(i).wait_send()

    @pl.when((odd_pair == 1) & (ctx < places - 4))
    def _():
        for i in range(turns):
            leap_copy(i).wait_send()

    def drain(s, carry):
        piece_copy(0, s).wait_send()
        piece_copy(1, s).wait_send()
        leave(s).wait()
        square_near(s).wait_send()
        far_copy(s).wait_send()
        square_far(s).wait_send()
        return carry

    lax.fori_loop(0, subs, drain, 0)

    @pl.when(ctx < places - 1)
    def _():
        for h in range(4):
            halo(h, me).wait_send()


def per_device(
    places,
    hidden,
    norm_gain,
    zx_weight,
    bc_weight,
    dt_weight,
    conv_x,
    conv_bc,
    dt_bias,
    log_decay,
    skip_gain,
    out_gain,
    out_weight,
):
    rows, feat = hidden.shape
    width = zx_weight.shape[0]
    inner = zx_weight.shape[2]
    turns = CUTS * inner // GROUP // 2
    tiles = inner // LANES
    chunks = rows // BLOCK
    subs = rows // SUB
    any_spec = pl.BlockSpec(memory_space=pl.ANY)
    vmem = pl.BlockSpec(memory_space=pltpu.VMEM)
    smem = pl.BlockSpec(memory_space=pltpu.SMEM)
    dma = pltpu.SemaphoreType.DMA
    return pl.pallas_call(
        functools.partial(kernel, places),
        out_shape=jax.ShapeDtypeStruct((rows, feat), BF16),
        in_specs=[any_spec] * 4 + [vmem] * 4 + [smem, vmem, smem, vmem],
        out_specs=any_spec,
        scratch_shapes=[
            pltpu.VMEM((4, HALO + rows, feat), BF16),
            pltpu.VMEM((tiles, width, 2, LANES), BF16),
            pltpu.VMEM((2, 2 * CUT, LANES), F32),
            pltpu.VMEM((width, 2 * inner), BF16),
            pltpu.VMEM((width, 2 * STATE), BF16),
            pltpu.VMEM((inner, width), BF16),
            pltpu.VMEM((width, 128), BF16),
            pltpu.VMEM((8, 128), F32),
            pltpu.VMEM((8, inner), F32),
            pltpu.VMEM((rows, width), BF16),
            pltpu.VMEM((HALO, inner + 2 * STATE), F32),
            pltpu.VMEM((16, BLOCK), F32),
            pltpu.VMEM((rows, inner), BF16),
            pltpu.VMEM((rows, STATE), BF16),
            pltpu.VMEM((rows, inner), F32),
            pltpu.VMEM((rows, inner), F32),
            pltpu.VMEM((chunks, STATE, inner), BF16),
            pltpu.VMEM((chunks, 8, inner), F32),
            pltpu.VMEM((chunks, 8, inner), F32),
            pltpu.VMEM((rows, 128), F32),
            pltpu.VMEM((128, inner), BF16),
            pltpu.VMEM((chunks, 16, BLOCK), F32),
            pltpu.VMEM((STATE, inner), F32),
            pltpu.VMEM((8, inner), F32),
            pltpu.VMEM((rows, STATE), BF16),
            pltpu.VMEM((chunks, 16, BLOCK), F32),
            pltpu.VMEM((8, inner), F32),
            pltpu.VMEM((8, inner), F32),
            pltpu.VMEM((8, inner), F32),
            pltpu.VMEM((turns, PIECE, GROUP), BF16),
            pltpu.VMEM((turns, PIECE, GROUP), BF16),
            pltpu.VMEM((turns, PIECE, GROUP), BF16),
            pltpu.VMEM((turns, PIECE, GROUP), BF16),
            pltpu.VMEM((turns, PIECE, GROUP), BF16),
            pltpu.VMEM((turns, PIECE, GROUP), BF16),
            pltpu.VMEM((turns, PIECE, GROUP), BF16),
            pltpu.VMEM((STATE, inner), BF16),
            pltpu.VMEM((SUB, inner), BF16),
            pltpu.VMEM((2, subs, SUB, feat), BF16),
            pltpu.VMEM((2, subs, SUB, feat), BF16),
            pltpu.VMEM((subs, SUB, feat), F32),
            pltpu.VMEM((subs, SUB, feat), F32),
            pltpu.VMEM((rows, feat), BF16),
            pltpu.VMEM((subs, SUB, feat), BF16),
            pltpu.VMEM((subs, SUB, feat), BF16),
            pltpu.VMEM((subs, 8, SUB), F32),
            pltpu.VMEM((subs, 8, SUB), F32),
            pltpu.VMEM((subs, 8, SUB), F32),
            pltpu.VMEM((subs, 8, SUB), F32),
            dma((6 + tiles,)),
            dma((chunks,)),
            dma((chunks,)),
            dma((chunks,)),
            dma((chunks,)),
            dma((chunks,)),
            dma((chunks,)),
            dma((4,)),
            dma((4,)),
            dma((2,)),
            dma((2,)),
            dma((turns,)),
            dma((turns,)),
            dma((turns,)),
            dma((turns,)),
            dma((turns,)),
            dma((turns,)),
            dma((turns,)),
            dma((turns,)),
            dma((2, subs)),
            dma((2, subs)),
            dma((subs,)),
            dma((subs,)),
            dma((2, subs)),
            dma((2, subs)),
            dma((subs,)),
        ],
        compiler_params=pltpu.CompilerParams(
            collective_id=0, has_side_effects=True, vmem_limit_bytes=63000000
        ),
        name="mixer",
    )(
        hidden,
        zx_weight,
        bc_weight,
        out_weight,
        norm_gain,
        dt_weight.T,
        conv_x,
        conv_bc,
        dt_bias,
        log_decay.T,
        skip_gain,
        out_gain,
    )


def solution(mesh):
    placed = (
        P("ctx", "head"),
        P(),
        P(None, None, "head"),
        P(),
        P(None, "head"),
        P(None, "head"),
        P(),
        P("head"),
        P("ctx", "head"),
        P("head"),
        P("head"),
        P("head", None),
    )
    return jax.shard_map(
        functools.partial(per_device, mesh.shape["ctx"]),
        mesh=mesh,
        in_specs=placed,
        out_specs=P("ctx", "head"),
        check_vma=False,
    )
```
